1024 devices in a mesh: sub: 64 (over y, x, core), rep: 16 (over z).
Axes of the slice: x: 4, y: 8, z: 16, core: 2. Of those that a mesh axis runs over, the one named last changes fastest.
Arguments:
- dual_ops: bfloat16 [1024, 1024, 1024], P(('sub', 'rep'))
- mode_traces: float32 [1024, 6, 1024], P(('sub', 'rep')), may hold values from -0.046875 to 0.046875
- route: int32 [1024, 1024], P(('sub', 'rep')), may hold values from 0 to 1023, each once within a row
- mode_block: int32 [1024, 1], replicated, may hold values from 0 to 63
- local_gap: float32 [32, 1048576], P(None, ('sub', 'rep')), may hold values from -6 to 6
Outputs:
- multipliers: float32 [32, 1048576], P(None, ('sub', 'rep'))
- amplitudes: float32 [32, 384], replicated
The draws below stay inside these ranges and needn't reach their ends.
Inputs may be any that keep to these rules, and one draw needn't show every extreme that they name: Each row of route lists every number below 1024 once. `mode_block`: every aggregate holds at least one subdomain.
All inputs are finite; a program needn't handle non-finite values.
Results may differ from the reference program's by a relative error of at most 0.003.
Values sent between devices are 32-bit elements; how exact they have to be, the bound alone decides.
A program may use at most 32 MiB of HBM per device.

```python
import math
import jax
import jax.numpy as jnp
from jax import lax

B = 1024
R = 32
MODES = 6
AGG_SUBS = 16
ITERS = 2
SUBS = 1024
ROWS = 1048576
MODE_BLOCKS = 64
NC = 384
N_SUB = 64
N_REP = 16


def draw_dual_ops(key, part):
    noise_key, diag_key, scale_key = jax.random.split(key, 3)
    noise_draw = jax.random.uniform(noise_key, (SUBS, B, B), jnp.float32, -1.0, 1.0)
    symmetric = 0.5 * (noise_draw + jnp.swapaxes(noise_draw, 1, 2))
    diagonal = jnp.exp(jax.random.uniform(diag_key, (SUBS, B), jnp.float32, math.log(2.0), math.log(4.0)))
    stiffness = jnp.exp(jax.random.uniform(scale_key, (SUBS, 1, 1), jnp.float32, math.log(0.5), math.log(2.0)))
    identity = jnp.eye(B, dtype=jnp.float32)
    matrix = symmetric * (1.8 / math.sqrt(B)) * (1.0 - identity) + identity * diagonal[:, None, :]
    return (stiffness * matrix).astype(jnp.bfloat16)


def shard_levels(stream_key, extent, cuts, low, largest):
    level, own = 1.0, jax.random.fold_in(stream_key, 6)
    for axis_at, blocks in cuts:
        heights = jnp.exp(jax.random.uniform(jax.random.fold_in(own, axis_at), (blocks,), jnp.float32, low / len(cuts), largest / len(cuts)))
        level = level * jnp.repeat(heights, extent[axis_at] // blocks).reshape([-1 if axis == axis_at else 1 for axis in range(len(extent))])
    return level


def distinct(rng, rows, amount, top, lift):
    order = jax.random.permutation(jax.random.fold_in(rng, 1), amount)
    pull = order
    for power in range(3):
        pull = pull * pull // amount
    pull = pull * lift // amount
    lots = jax.random.randint(jax.random.fold_in(rng, 2), (rows, amount), 0, 4096) + pull
    sure = jax.random.permutation(jax.random.fold_in(rng, 3), rows)[jnp.arange(amount) % rows]
    lots = jnp.where(jnp.arange(rows)[:, None] == sure[None, :], 1 << 14, lots)
    merit = lots * amount + jnp.arange(amount)
    return lax.top_k(merit.astype(jnp.int32), top)[1].astype(jnp.int32)


def gaussian(own_key, dims, scale, reach, cuts=(), kind=jnp.bfloat16):
    entries = scale * jax.random.normal(own_key, dims, jnp.float32)
    if cuts:
        entries = entries * shard_levels(own_key, dims, cuts, -0.22, 0.18)
    return jnp.clip(entries, -reach, reach).astype(kind)


def setup_inputs(seed: int = 0) -> dict:
    key_of = jax.random.split(jax.random.key(seed), 6)
    return {
        "dual_ops": draw_dual_ops(jax.random.fold_in(key_of[5], 71), 0),
        "mode_traces": gaussian(key_of[1], (SUBS, MODES, B), (AGG_SUBS * B) ** -0.5, 0.046875, ((0, 1024),), jnp.float32),
        "route": jax.vmap(lambda own: jax.random.permutation(own, B))(jax.random.split(key_of[2], SUBS)).reshape((SUBS, B)).astype(jnp.int32),
        "mode_block": distinct(key_of[3], SUBS, MODE_BLOCKS, 1, 0),
        "local_gap": gaussian(key_of[4], (R, ROWS), 1.0, 6.0, ((1, 1024),), jnp.float32),
    }


HIGHEST = lax.Precision.HIGHEST

def reference(dual_ops, mode_traces, route, mode_block, local_gap):
    per_peer = B // N_SUB
    slot_local = route.reshape(N_SUB, N_REP, N_SUB, per_peer)
    row_base = (jnp.arange(N_SUB, dtype=jnp.int32)[:, None] * N_REP + jnp.arange(N_REP, dtype=jnp.int32)[None, :]) * B
    rows_at = (slot_local + row_base[:, :, None, None]).astype(jnp.int32)
    swapped = jnp.transpose(rows_at, (2, 1, 0, 3))
    on_diagonal = (jnp.arange(N_SUB)[:, None] == jnp.arange(N_SUB)[None, :])[:, None, :, None]
    partner_at = jnp.where(on_diagonal, jnp.flip(swapped, 3), swapped).astype(jnp.int32)
    partner = jnp.zeros((ROWS,), jnp.int32).at[rows_at.reshape(-1)].set(partner_at.reshape(-1))

    def jump_of(values):
        return values - values[:, partner]
    blocks = mode_block[:, 0]
    labels = jnp.arange(MODE_BLOCKS, dtype=jnp.int32)
    onehot = (blocks[:, None] == labels[None, :]).astype(jnp.float32)

    def coarse_term(values):
        shaped = values.reshape(R, SUBS, B)
        per_sub = 2.0 * jnp.einsum('nkb,rnb->rnk', mode_traces, shaped, precision=HIGHEST)
        return jnp.einsum('na,rnk->rak', onehot, per_sub, precision=HIGHEST).reshape(R, NC)

    def expand(amounts):
        per_sub = jnp.einsum('na,rak->rnk', onehot, amounts.reshape(R, MODE_BLOCKS, MODES), precision=HIGHEST)
        spread = jnp.einsum('nkb,rnk->rnb', mode_traces, per_sub, precision=HIGHEST)
        return jump_of(spread.reshape(R, ROWS))
    row_traces = jnp.transpose(mode_traces, (0, 2, 1)).reshape(ROWS, MODES)
    row_blocks = jnp.repeat(blocks, B)
    far_traces = row_traces[partner].reshape(SUBS, B, MODES)
    far_blocks = row_blocks[partner].reshape(SUBS, B)

    def cross_row(pieces):
        traces_one, far_traces_one, far_blocks_one = pieces
        hits = (far_blocks_one[:, None] == labels[None, :]).astype(jnp.float32)
        embedded = (hits[:, :, None] * far_traces_one[:, None, :]).reshape(B, NC)
        return jnp.dot(traces_one, embedded, precision=HIGHEST)
    cross_terms = lax.map(cross_row, (mode_traces, far_traces, far_blocks))
    own_gram = jnp.einsum('nkb,nlb->nkl', mode_traces, mode_traces, precision=HIGHEST)
    own_rows = (own_gram[:, :, None, :] * onehot[:, None, :, None]).reshape(SUBS, MODES, NC)
    gram_matrix = jnp.einsum('na,nkc->akc', onehot, 2.0 * (own_rows - cross_terms), precision=HIGHEST).reshape(NC, NC)
    factor = jnp.linalg.cholesky(gram_matrix)

    def solve_coarse(right):
        return jax.scipy.linalg.cho_solve((factor, True), right.T).T

    def product_one(pieces):
        return lax.dot_general(pieces[1].astype(jnp.float32), pieces[0].astype(jnp.float32), (((1,), (1,)), ((), ())), preferred_element_type=jnp.float32)

    def apply_ops(values):
        shaped = jnp.transpose(values.reshape(R, SUBS, B).astype(jnp.bfloat16), (1, 0, 2))
        result = lax.map(product_one, (dual_ops, shaped))
        return jnp.transpose(result, (1, 0, 2)).reshape(R, ROWS)
    residual = jump_of(local_gap)
    amplitudes = solve_coarse(coarse_term(residual))
    projected = residual - expand(amplitudes)
    inner_sum = jnp.sum(projected * projected, axis=1)
    direction = projected
    multipliers = jnp.zeros_like(residual)
    for iteration in range(ITERS):
        product = apply_ops(direction)
        image_jump = jump_of(product)
        step_size = inner_sum / jnp.sum(direction * image_jump, axis=1)
        multipliers = multipliers + step_size[:, None] * direction
        residual = residual - step_size[:, None] * image_jump
        amplitudes = solve_coarse(coarse_term(residual))
        if iteration + 1 < ITERS:
            projected = residual - expand(amplitudes)
            renewed = jnp.sum(projected * projected, axis=1)
            direction = projected + (renewed / inner_sum)[:, None] * direction
            inner_sum = renewed
    return (multipliers, amplitudes)
```

```python
import jax
import jax.numpy as jnp
from jax import lax
from jax.experimental import pallas as pl
from jax.experimental.pallas import tpu as pltpu
from jax.sharding import PartitionSpec as P

SUB = 64
REP = 16
PER = 16
ROWS = 1024
CASES = 32
MODES = 6
AGGS = 64
NC = 384
TILES = 16
SLICE = 24
HALF = 24
F32 = jnp.float32
BF16 = jnp.bfloat16
HIGHEST = lax.Precision.HIGHEST
MESH = pl.DeviceIdType.MESH


def nt(left, right, precision=None):
    return lax.dot_general(
        left, right, (((1,), (1,)), ((), ())), precision=precision, preferred_element_type=F32
    )


def nn(left, right, precision=None):
    return lax.dot_general(
        left, right, (((1,), (0,)), ((), ())), precision=precision, preferred_element_type=F32
    )


def split(values):
    high = values.astype(BF16)
    rest = values - high.astype(F32)
    middle = rest.astype(BF16)
    low = (rest - middle.astype(F32)).astype(BF16)
    return high, middle, low


def permuted(values, onehot, product):
    high, middle, low = split(values)
    return (product(high, onehot) + product(middle, onehot)) + product(low, onehot)


def iota(shape, dim):
    return lax.broadcasted_iota(jnp.int32, shape, dim)


def greet(own, plane):
    barrier = pltpu.get_barrier_semaphore()

    def over_sub(i, _):
        pl.semaphore_signal(
            barrier, inc=1, device_id=(lax.rem(own + i, SUB), plane), device_id_type=MESH
        )
        return 0

    def over_rep(i, _):
        pl.semaphore_signal(
            barrier, inc=1, device_id=(own, lax.rem(plane + i, REP)), device_id_type=MESH
        )
        return 0

    lax.fori_loop(1, SUB, over_sub, 0)
    lax.fori_loop(1, REP, over_rep, 0)
    return barrier


def to_peer(source, target, send, receive, peer, plane):
    return pltpu.make_async_remote_copy(
        src_ref=source,
        dst_ref=target,
        send_sem=send,
        recv_sem=receive,
        device_id=(peer, plane),
        device_id_type=MESH,
    )


def pack(values, message_ref):
    wide = jnp.concatenate([values, jnp.zeros((64, ROWS), F32)], axis=0)
    tall = jnp.transpose(wide).reshape(SUB, 2, 8, 128)
    message_ref[...] = tall[:, 0] + pltpu.roll(tall[:, 1], 64, 2)


def unpack(landed_ref):
    tiles = landed_ref[...]
    low = iota((SUB, 8, 128), 2) < 64
    first = jnp.where(low, tiles, 0.0)
    second = jnp.where(low, pltpu.roll(tiles, 64, 2), 0.0)
    tall = jnp.stack([first, second], axis=1).reshape(ROWS, 128)
    return jnp.transpose(tall)[:64]


def flip_own(message_ref, landed_ref, own):
    tile = pltpu.roll(message_ref[own], 64, 1)
    for a in range(8):
        landed_ref[own, pl.ds(7 - a, 1), :] = tile[a : a + 1, :]


def exchange_start(message_ref, landed_ref, send, receive, own, plane):
    def one(i, _):
        peer = lax.rem(own + i, SUB)
        to_peer(
            message_ref.at[peer], landed_ref.at[own], send.at[peer], receive.at[own], peer, plane
        ).start()
        return 0

    lax.fori_loop(1, SUB, one, 0)


def exchange_wait(message_ref, landed_ref, send, receive, own, plane):
    def one(i, _):
        peer = lax.rem(own + i, SUB)
        to_peer(
            message_ref.at[peer], landed_ref.at[peer], send.at[peer], receive.at[peer], peer, plane
        ).wait_recv()
        return 0

    lax.fori_loop(1, SUB, one, 0)


def exchange_sent(message_ref, landed_ref, send, receive, own, plane):
    def one(i, _):
        peer = lax.rem(own + i, SUB)
        to_peer(
            message_ref.at[peer], landed_ref.at[peer], send.at[peer], receive.at[peer], peer, plane
        ).wait_send()
        return 0

    lax.fori_loop(1, SUB, one, 0)


def spread_start(piece_ref, landed_ref, index, send, receive, own, plane):
    def one(i, _):
        peer = lax.rem(own + i, SUB)
        to_peer(
            piece_ref, landed_ref.at[index], send.at[peer], receive.at[index], peer, plane
        ).start()
        return 0

    lax.fori_loop(1, SUB, one, 0)


def spread_sent(piece_ref, landed_ref, index, send, receive, own, plane):
    def one(i, _):
        peer = lax.rem(own + i, SUB)
        to_peer(
            piece_ref, landed_ref.at[index], send.at[peer], receive.at[index], peer, plane
        ).wait_send()
        return 0

    lax.fori_loop(1, SUB, one, 0)


def column(piece_ref, landed_ref, send, receive, own, plane, act):
    def one(i, _):
        other = lax.rem(plane + i, REP)
        if act == "start":
            to_peer(
                piece_ref, landed_ref.at[plane], send.at[other], receive.at[plane], own, other
            ).start()
        elif act == "recv":
            to_peer(
                piece_ref, landed_ref.at[other], send.at[other], receive.at[other], own, other
            ).wait_recv()
        else:
            to_peer(
                piece_ref, landed_ref.at[other], send.at[other], receive.at[other], own, other
            ).wait_send()
        return 0

    lax.fori_loop(1, REP, one, 0)


def setup_kernel(
    operator_ref, traces_ref, route_ref, blocks_ref, gap_ref,
    residual_ref, basis_ref, glued_ref, onehot_ref, gram_ref, coarse_ref, norm_ref,
    message, landed, rows_ref, half_ref, pair_ref, even_ref,
    gram_out, gram_in, part_ref, column_in, total_ref, gathered,
    send_a, receive_a, send_b, receive_b, send_c, receive_c, send_d, receive_d,
):
    own = lax.axis_index("sub")
    plane = lax.axis_index("rep")
    barrier = greet(own, plane)

    route_row = route_ref[...]
    wide_route = jnp.broadcast_to(route_row, (128, ROWS)).astype(F32)

    @pl.loop(0, 4)
    def _(step):
        rows = pl.ds(pl.multiple_of(step * 256, 256), 256)
        hit = iota((256, ROWS), 0) + step * 256 == route_row
        onehot_ref[rows, :] = hit.astype(F32).astype(BF16)

    stacked = jnp.concatenate(
        [gap_ref[...], traces_ref[0], jnp.zeros((2, ROWS), F32)], axis=0
    )
    ordered = permuted(stacked, onehot_ref[...], nn)
    pack(jnp.concatenate([ordered, jnp.zeros((24, ROWS), F32)], axis=0), message)

    pl.semaphore_wait(barrier, SUB - 1 + REP - 1)
    exchange_start(message, landed, send_a, receive_a, own, plane)
    flip_own(message, landed, own)

    tall_route = jnp.transpose(wide_route)
    for tile in range(8):
        hit = tall_route == (iota((ROWS, 128), 1) + tile * 128).astype(F32)
        rows_ref[:, tile * 128 : tile * 128 + 128] = hit.astype(F32).astype(BF16)

    @pl.loop(0, 4)
    def _(step):
        rows = pl.ds(pl.multiple_of(step * 256, 256), 256)
        half_ref[rows, :] = nn(operator_ref[0, rows, :], onehot_ref[...]).astype(BF16)

    @pl.loop(0, 4)
    def _(step):
        rows = pl.ds(pl.multiple_of(step * 256, 256), 256)
        glued_ref[rows, :] = nn(rows_ref[rows, :], half_ref[...]).astype(BF16)

    blocks = blocks_ref[...].astype(F32)
    picked = jnp.where(iota((SUB, REP), 1) == plane, blocks, 0.0)
    peer_block = jnp.sum(picked, axis=1, keepdims=True)
    hit = peer_block == iota((SUB, 128), 1).astype(F32)
    by_peer = jnp.concatenate([hit.astype(F32), jnp.zeros((64, 128), F32)], axis=0)
    by_block = jnp.transpose(by_peer)
    repeat = (iota((128, ROWS), 1) // PER == iota((128, ROWS), 0)).astype(F32).astype(BF16)
    peer_mask = nn(by_block[:AGGS].astype(BF16), repeat)
    own_mask = jnp.sum(
        jnp.where(iota((AGGS, 128), 1) == own, by_block[:AGGS], 0.0), axis=1, keepdims=True
    )
    traces = ordered[CASES : CASES + 8]
    pair_ref[...] = jnp.zeros_like(pair_ref)
    even_ref[...] = jnp.zeros_like(even_ref)
    for k in range(MODES):
        row = traces[k : k + 1]
        at = k // 2 + HALF * (k % 2)
        even_ref[at : at + 1, :] = row
        lane = (18, 42, 19)[k // 2]
        pair_ref[k % 2, lane : lane + 1, :] = row

    exchange_wait(message, landed, send_a, receive_a, own, plane)
    partner = unpack(landed)
    residual = ordered[:CASES] - partner[:CASES]
    residual_ref[...] = residual
    for k in range(MODES):
        basis_ref[64 * k : 64 * k + 64, :] = (
            own_mask * traces[k : k + 1] - peer_mask * partner[CASES + k : CASES + k + 1]
        )
    crossed = 2.0 * nt(basis_ref[...], even_ref[...], HIGHEST)
    outgoing = crossed[:64]
    for k in range(1, MODES):
        outgoing = outgoing + pltpu.roll(crossed[64 * k : 64 * k + 64], 3 * k, 1)
    first = 2.0 * nt(residual, pair_ref[0], HIGHEST)
    second = 2.0 * nt(residual, pair_ref[1], HIGHEST)
    squares = jnp.sum(residual * residual, axis=1, keepdims=True)
    first = jnp.where(iota((CASES, 128), 1) == 43, squares, first)
    gram_out[...] = (outgoing + jnp.concatenate([first, second], axis=0)).reshape(SUB, 1, 128)

    exchange_start(gram_out, gram_in, send_b, receive_b, own, plane)
    gram_in[own] = gram_out[own]
    exchange_sent(message, landed, send_a, receive_a, own, plane)
    exchange_wait(gram_out, gram_in, send_b, receive_b, own, plane)
    arrived = gram_in[...].reshape(SUB, 128)
    turned = jnp.transpose(jnp.concatenate([arrived, jnp.zeros((64, 128), F32)], axis=0))
    grouped = nn(turned[: 2 * HALF], by_peer, HIGHEST)
    part_ref[...] = grouped[:HALF] + pltpu.roll(grouped[HALF:], 64, 1)

    column(part_ref, column_in, send_c, receive_c, own, plane, "start")
    column_in[plane] = part_ref[...]
    exchange_sent(gram_out, gram_in, send_b, receive_b, own, plane)
    column(part_ref, column_in, send_c, receive_c, own, plane, "recv")
    total_ref[...] = jnp.sum(column_in[...], axis=0)

    spread_start(total_ref, gathered, own, send_d, receive_d, own, plane)
    gathered[own] = total_ref[...]
    column(part_ref, column_in, send_c, receive_c, own, plane, "sent")
    exchange_wait(gathered, gathered, send_d, receive_d, own, plane)
    for k in range(MODES):
        for j in range(3):
            gram_ref[64 * k : 64 * k + 64, 128 * j : 128 * j + 128] = gathered[:, 3 * k + j, :]
    near = gathered[:, 18, :]
    far = gathered[:, 19, :]
    even_odd = (near, pltpu.roll(near, 64, 1), far)
    lower = iota((CASES, 128), 1) < 64
    for i in range(3):
        coarse_ref[:, 128 * i : 128 * i + 128] = jnp.where(
            lower, even_odd[i][:CASES], pltpu.roll(even_odd[i][CASES:], 64, 1)
        )
    totals = jnp.sum(jnp.where(iota((CASES, 128), 1) >= 64, far[:CASES], 0.0), axis=1, keepdims=True)
    norm_ref[...] = jnp.broadcast_to(totals, (CASES, 128))
    spread_sent(total_ref, gathered, own, send_d, receive_d, own, plane)


def invert_kernel(gram_ref, inverse_ref):
    inverse_ref[...] = gram_ref[...]
    lane = iota((128, 128), 1)
    line = iota((128, 128), 0)

    @pl.loop(0, 3)
    def _(block):
        at = pl.ds(pl.multiple_of(block * 128, 128), 128)
        pivot = inverse_ref[at, at]
        for k in range(128):
            scale = 1.0 / pivot[k : k + 1, k : k + 1]
            row = jnp.where(lane[:1] == k, scale, pivot[k : k + 1, :] * scale)
            left = pivot[:, k : k + 1]
            kept = jnp.where(lane == k, 0.0, pivot)
            pivot = jnp.where(line == k, row, kept - left * row)
        rows = nn(pivot, inverse_ref[at, :], HIGHEST)
        lefts = inverse_ref[:, at]
        mine = iota((NC, 128), 0) // 128 == block
        lefts = jnp.where(mine, 0.0, lefts)
        inverse_ref[...] = inverse_ref[...] - nn(lefts, rows, HIGHEST)
        inverse_ref[:, at] = -nn(lefts, pivot, HIGHEST)
        inverse_ref[at, :] = rows
        inverse_ref[at, at] = pivot


def owner_of(tile):
    return 4 * tile + lax.rem(tile, 4)


def reduce_start(pay, first_in, send, receive, own, plane):
    def one(tile, _):
        peer = owner_of(tile)

        @pl.when(peer != own)
        def _():
            to_peer(
                pay.at[tile], first_in.at[own], send.at[tile], receive.at[own], peer, plane
            ).start()

        return 0

    lax.fori_loop(0, TILES, one, 0)


def reduce_middle(pay, first_in, mid, second_in, last, result, sems, own, plane):
    send_1, receive_1, send_2, receive_2, send_3, receive_3 = sems
    tile = own // 4

    @pl.when(lax.rem(own, 4) == lax.rem(tile, 4))
    def _():
        first_in[own] = pay[tile]

        def one(i, _):
            peer = lax.rem(own + i, SUB)
            to_peer(
                pay.at[tile], first_in.at[peer], send_1.at[tile], receive_1.at[peer], peer, plane
            ).wait_recv()
            return 0

        lax.fori_loop(1, SUB, one, 0)
        mid[...] = jnp.sum(first_in[...], axis=0)
        column(mid, second_in, send_2, receive_2, own, plane, "start")
        second_in[plane] = mid[...]
        column(mid, second_in, send_2, receive_2, own, plane, "recv")
        last[...] = jnp.sum(second_in[...], axis=0)
        spread_start(last, result, tile, send_3, receive_3, own, plane)
        result[tile] = last[...]


def reduce_finish(pay, first_in, mid, second_in, last, result, sems, own, plane):
    send_1, receive_1, send_2, receive_2, send_3, receive_3 = sems

    def one(tile, _):
        peer = owner_of(tile)

        @pl.when(peer != own)
        def _():
            to_peer(
                last, result.at[tile], send_3.at[peer], receive_3.at[tile], peer, plane
            ).wait_recv()

        return 0

    lax.fori_loop(0, TILES, one, 0)


def reduce_sent(pay, first_in, mid, second_in, last, result, sems, own, plane):
    send_1, receive_1, send_2, receive_2, send_3, receive_3 = sems

    def one(tile, _):
        peer = owner_of(tile)

        @pl.when(peer != own)
        def _():
            to_peer(
                pay.at[tile], first_in.at[own], send_1.at[tile], receive_1.at[own], peer, plane
            ).wait_send()

        return 0

    lax.fori_loop(0, TILES, one, 0)
    tile = own // 4

    @pl.when(lax.rem(own, 4) == lax.rem(tile, 4))
    def _():
        column(mid, second_in, send_2, receive_2, own, plane, "sent")
        spread_sent(last, result, tile, send_3, receive_3, own, plane)


def load_pay(pay, sums, scalars):
    extra = jnp.zeros((CASES, 128), F32)
    for at, value in enumerate(scalars):
        extra = jnp.where(iota((CASES, 128), 1) == at, value, extra)
    for i in range(4):
        for j in range(3):
            pay[4 * i + j] = sums[8 * i : 8 * i + 8, 128 * j : 128 * j + 128]
        pay[4 * i + 3] = extra[8 * i : 8 * i + 8]


def read_result(result):
    columns = []
    for j in range(4):
        columns.append(jnp.concatenate([result[4 * i + j] for i in range(4)], axis=0))
    return jnp.concatenate(columns[:3], axis=1), columns[3]


def row_sum(values):
    return jnp.sum(values, axis=1, keepdims=True)


def solve_kernel(
    residual_ref, basis_ref, glued_ref, onehot_ref, inverse_ref, coarse_ref, norm_ref,
    multipliers_ref, amplitudes_ref,
    message, landed, pay_a, first_a, mid_a, second_a, last_a, result_a,
    pay_b, first_b, mid_b, second_b, last_b, result_b,
    send_x, receive_x,
    send_a1, receive_a1, send_a2, receive_a2, send_a3, receive_a3,
    send_b1, receive_b1, send_b2, receive_b2, send_b3, receive_b3,
):
    own = lax.axis_index("sub")
    plane = lax.axis_index("rep")
    barrier = greet(own, plane)
    round_a = (pay_a, first_a, mid_a, second_a, last_a, result_a,
               (send_a1, receive_a1, send_a2, receive_a2, send_a3, receive_a3), own, plane)
    round_b = (pay_b, first_b, mid_b, second_b, last_b, result_b,
               (send_b1, receive_b1, send_b2, receive_b2, send_b3, receive_b3), own, plane)

    residual = residual_ref[...]
    coarse = coarse_ref[...]
    start = nn(coarse, inverse_ref[...], HIGHEST)
    direction = residual - nn(start, basis_ref[...], HIGHEST)
    inner = norm_ref[:, :1] - row_sum(start * coarse)
    product = nt(direction.astype(BF16), glued_ref[...])
    pack(jnp.concatenate([product, jnp.zeros((32, ROWS), F32)], axis=0), message)
    load_pay(pay_a, 2.0 * nt(product, basis_ref[...], HIGHEST), (2.0 * row_sum(direction * product),))

    pl.semaphore_wait(barrier, SUB - 1 + REP - 1)
    reduce_start(pay_a, first_a, send_a1, receive_a1, own, plane)
    exchange_start(message, landed, send_x, receive_x, own, plane)
    flip_own(message, landed, own)
    reduce_middle(*round_a)
    exchange_wait(message, landed, send_x, receive_x, own, plane)
    jumped = product - unpack(landed)[:CASES]
    reduce_finish(*round_a)

    coarse_jump, sums = read_result(result_a)
    curvature = sums[:, 0:1]
    step = inner / curvature
    coarse_next = coarse - step * coarse_jump
    amplitudes = nn(coarse_next, inverse_ref[...], HIGHEST)
    projected = (residual - step * jumped) - nn(amplitudes, basis_ref[...], HIGHEST)
    high, low, _ = split(projected)
    both = nt(jnp.concatenate([high, low], axis=0), glued_ref[...])
    image = both[:CASES] + both[CASES:]
    load_pay(
        pay_b,
        2.0 * nt(image, basis_ref[...], HIGHEST),
        (
            2.0 * row_sum(projected * image),
            2.0 * row_sum(projected * product) + 2.0 * row_sum(direction * image),
            row_sum(projected * projected),
        ),
    )
    reduce_start(pay_b, first_b, send_b1, receive_b1, own, plane)
    reduce_middle(*round_b)
    direction_rows = permuted(direction, onehot_ref[...], nt)
    projected_rows = permuted(projected, onehot_ref[...], nt)
    order = (
        iota((NC, NC), 1)
        == MODES * jnp.bitwise_and(iota((NC, NC), 0), AGGS - 1) + lax.shift_right_logical(iota((NC, NC), 0), 6)
    ).astype(F32).astype(BF16)
    exchange_sent(message, landed, send_x, receive_x, own, plane)
    reduce_sent(*round_a)
    reduce_finish(*round_b)

    image_coarse, sums = read_result(result_b)
    renewed = sums[:, 2:3]
    ratio = renewed / inner
    bend = sums[:, 0:1] + ratio * sums[:, 1:2] + ratio * ratio * curvature
    step_next = renewed / bend
    coarse_last = coarse_next - step_next * (image_coarse + ratio * coarse_jump)
    final = nn(coarse_last, inverse_ref[...], HIGHEST)
    amplitudes_ref[...] = permuted(final, order, nn)
    multipliers_ref[...] = (
        step * direction_rows + step_next * (projected_rows + ratio * direction_rows)
    )
    reduce_sent(*round_b)


VMEM = pl.BlockSpec(memory_space=pltpu.VMEM)
DMA = pltpu.SemaphoreType.DMA


def shape(dims, kind=F32):
    return jax.ShapeDtypeStruct(dims, kind)


def body(dual_ops, mode_traces, route, mode_block, local_gap):
    blocks = mode_block.reshape(SUB, REP)
    residual, basis, glued, onehot, gram, coarse, norm = pl.pallas_call(
        setup_kernel,
        out_shape=(
            shape((CASES, ROWS)), shape((NC, ROWS)), shape((ROWS, ROWS), BF16),
            shape((ROWS, ROWS), BF16), shape((NC, NC)), shape((CASES, NC)), shape((CASES, 128)),
        ),
        in_specs=[VMEM] * 5,
        out_specs=(VMEM,) * 7,
        scratch_shapes=[
            pltpu.VMEM((SUB, 8, 128), F32), pltpu.VMEM((SUB, 8, 128), F32),
            pltpu.VMEM((ROWS, ROWS), BF16), pltpu.VMEM((ROWS, ROWS), BF16),
            pltpu.VMEM((2, 128, ROWS), F32), pltpu.VMEM((128, ROWS), F32),
            pltpu.VMEM((SUB, 1, 128), F32), pltpu.VMEM((SUB, 1, 128), F32),
            pltpu.VMEM((SLICE, 128), F32), pltpu.VMEM((REP, SLICE, 128), F32),
            pltpu.VMEM((SLICE, 128), F32), pltpu.VMEM((SUB, SLICE, 128), F32),
            DMA((SUB,)), DMA((SUB,)), DMA((SUB,)), DMA((SUB,)),
            DMA((REP,)), DMA((REP,)), DMA((SUB,)), DMA((SUB,)),
        ],
        compiler_params=pltpu.CompilerParams(
            collective_id=0, has_side_effects=True, vmem_limit_bytes=48 * 1024 * 1024
        ),
        name="setup",
    )(dual_ops, mode_traces, route, blocks, local_gap)
    inverse = pl.pallas_call(
        invert_kernel,
        out_shape=shape((NC, NC)),
        in_specs=[VMEM],
        out_specs=VMEM,
        name="invert",
    )(gram)
    tile = pltpu.VMEM((8, 128), F32)
    many = pltpu.VMEM((SUB, 8, 128), F32)
    few = pltpu.VMEM((TILES, 8, 128), F32)
    return pl.pallas_call(
        solve_kernel,
        out_shape=(shape((CASES, ROWS)), shape((CASES, NC))),
        in_specs=[VMEM] * 7,
        out_specs=(VMEM,) * 2,
        scratch_shapes=[many, many] + [few, many, tile, few, tile, few] * 2
        + [DMA((SUB,)), DMA((SUB,))]
        + [DMA((TILES,)), DMA((SUB,)), DMA((REP,)), DMA((REP,)), DMA((SUB,)), DMA((TILES,))] * 2,
        compiler_params=pltpu.CompilerParams(
            collective_id=1, has_side_effects=True, vmem_limit_bytes=48 * 1024 * 1024
        ),
        name="solve",
    )(residual, basis, glued, onehot, inverse, coarse, norm)


def solution(mesh):
    placed = (
        P(("sub", "rep"), None, None),
        P(("sub", "rep"), None, None),
        P(("sub", "rep"), None),
        P(),
        P(None, ("sub", "rep")),
    )
    return jax.shard_map(
        body, mesh=mesh, in_specs=placed, out_specs=(P(None, ("sub", "rep")), P()), check_vma=False
    )
```

```python
import jax
import jax.numpy as jnp
from jax import lax
from jax.experimental import pallas as pl
from jax.experimental.pallas import tpu as pltpu
from jax.sharding import PartitionSpec as P

SUB = 64
REP = 16
PER = 16
ROWS = 1024
CASES = 32
MODES = 6
AGGS = 64
NC = 384
TILES = 16
SLICE = 24
HALF = 24
LIMIT = 24 * 1024 * 1024
F32 = jnp.float32
BF16 = jnp.bfloat16
HIGHEST = lax.Precision.HIGHEST
MESH = pl.DeviceIdType.MESH


def nt(left, right, precision=None):
    return lax.dot_general(
        left, right, (((1,), (1,)), ((), ())), precision=precision, preferred_element_type=F32
    )


def nn(left, right, precision=None):
    return lax.dot_general(
        left, right, (((1,), (0,)), ((), ())), precision=precision, preferred_element_type=F32
    )


def split(values):
    high = values.astype(BF16)
    rest = values - high.astype(F32)
    middle = rest.astype(BF16)
    low = (rest - middle.astype(F32)).astype(BF16)
    return high, middle, low


def stacked(values):
    return jnp.concatenate(split(values), axis=0)


def permuted(values, onehot, product):
    rows = values.shape[0]
    parts = product(stacked(values), onehot)
    return (parts[:rows] + parts[rows : 2 * rows]) + parts[2 * rows :]


def row_sum(values):
    return jnp.sum(values, axis=1, keepdims=True)


def iota(shape, dim):
    return lax.broadcasted_iota(jnp.int32, shape, dim)


def greet(own, plane):
    barrier = pltpu.get_barrier_semaphore()

    def over_sub(i, _):
        pl.semaphore_signal(
            barrier, inc=1, device_id=(lax.rem(own + i, SUB), plane), device_id_type=MESH
        )
        return 0

    def over_rep(i, _):
        pl.semaphore_signal(
            barrier, inc=1, device_id=(own, lax.rem(plane + i, REP)), device_id_type=MESH
        )
        return 0

    lax.fori_loop(1, SUB, over_sub, 0)
    lax.fori_loop(1, REP, over_rep, 0)
    return barrier


def to_peer(source, target, send, receive, peer, plane):
    return pltpu.make_async_remote_copy(
        src_ref=source,
        dst_ref=target,
        send_sem=send,
        recv_sem=receive,
        device_id=(peer, plane),
        device_id_type=MESH,
    )


def pack(values, message_ref):
    wide = jnp.concatenate([values, jnp.zeros((64, ROWS), F32)], axis=0)
    tall = jnp.transpose(wide).reshape(SUB, 2, 8, 128)
    message_ref[...] = tall[:, 0] + pltpu.roll(tall[:, 1], 64, 2)


def unpack(landed_ref):
    tiles = landed_ref[...]
    low = iota((SUB, 8, 128), 2) < 64
    first = jnp.where(low, tiles, 0.0)
    second = jnp.where(low, pltpu.roll(tiles, 64, 2), 0.0)
    tall = jnp.stack([first, second], axis=1).reshape(ROWS, 128)
    return jnp.transpose(tall)[:64]


def flip_own(message_ref, landed_ref, own):
    tile = pltpu.roll(message_ref[own], 64, 1)
    for a in range(8):
        landed_ref[own, pl.ds(7 - a, 1), :] = tile[a : a + 1, :]


def exchange_start(message_ref, landed_ref, send, receive, own, plane):
    def one(i, _):
        peer = lax.rem(own + i, SUB)
        to_peer(
            message_ref.at[peer], landed_ref.at[own], send.at[peer], receive.at[own], peer, plane
        ).start()
        return 0

    lax.fori_loop(1, SUB, one, 0)


def exchange_wait(message_ref, landed_ref, send, receive, own, plane):
    def one(i, _):
        peer = lax.rem(own + i, SUB)
        to_peer(
            message_ref.at[peer], landed_ref.at[peer], send.at[peer], receive.at[peer], peer, plane
        ).wait_recv()
        return 0

    lax.fori_loop(1, SUB, one, 0)


def exchange_sent(message_ref, landed_ref, send, receive, own, plane):
    def one(i, _):
        peer = lax.rem(own + i, SUB)
        to_peer(
            message_ref.at[peer], landed_ref.at[peer], send.at[peer], receive.at[peer], peer, plane
        ).wait_send()
        return 0

    lax.fori_loop(1, SUB, one, 0)


def spread_start(piece_ref, landed_ref, index, send, receive, own, plane):
    def one(i, _):
        peer = lax.rem(own + i, SUB)
        to_peer(
            piece_ref, landed_ref.at[index], send.at[peer], receive.at[index], peer, plane
        ).start()
        return 0

    lax.fori_loop(1, SUB, one, 0)


def spread_sent(piece_ref, landed_ref, index, send, receive, own, plane):
    def one(i, _):
        peer = lax.rem(own + i, SUB)
        to_peer(
            piece_ref, landed_ref.at[index], send.at[peer], receive.at[index], peer, plane
        ).wait_send()
        return 0

    lax.fori_loop(1, SUB, one, 0)


def column(piece_ref, landed_ref, send, receive, own, plane, act):
    def one(i, _):
        other = lax.rem(plane + i, REP)
        if act == "start":
            to_peer(
                piece_ref, landed_ref.at[plane], send.at[other], receive.at[plane], own, other
            ).start()
        elif act == "recv":
            to_peer(
                piece_ref, landed_ref.at[other], send.at[other], receive.at[other], own, other
            ).wait_recv()
        else:
            to_peer(
                piece_ref, landed_ref.at[other], send.at[other], receive.at[other], own, other
            ).wait_send()
        return 0

    lax.fori_loop(1, REP, one, 0)


def block_of(peer):
    return lax.rem(peer, 8) * 8 + peer // 8


def setup_kernel(
    operator_ref, traces_ref, route_ref, blocks_ref, gap_ref,
    residual_ref, modes_ref, mask_ref, own_ref, glued_ref, onehot_ref,
    gram_ref, coarse_ref, norm_ref,
    message, landed, rows_ref, half_ref,
    gram_out, gram_in, part_ref, column_in, total_ref, gathered,
    send_a, receive_a, send_b, receive_b, send_c, receive_c,
    send_d, receive_d, send_e, receive_e, send_f, receive_f,
):
    own = lax.axis_index("sub")
    plane = lax.axis_index("rep")
    barrier = greet(own, plane)

    route_row = route_ref[...]

    @pl.loop(0, 4)
    def _(step):
        rows = pl.ds(pl.multiple_of(step * 256, 256), 256)
        hit = iota((256, ROWS), 0) + step * 256 == route_row
        onehot_ref[rows, :] = hit.astype(F32).astype(BF16)

    natural = jnp.concatenate(
        [gap_ref[...]] + [traces_ref[k] for k in range(MODES)] + [jnp.zeros((10, ROWS), F32)],
        axis=0,
    )
    ordered = permuted(natural, onehot_ref[...], nn)
    pack(jnp.concatenate([ordered, jnp.zeros((16, ROWS), F32)], axis=0), message)

    pl.semaphore_wait(barrier, SUB - 1 + REP - 1)
    exchange_start(message, landed, send_a, receive_a, own, plane)
    flip_own(message, landed, own)

    repeat = (iota((128, ROWS), 1) // PER == iota((128, ROWS), 0)).astype(F32).astype(BF16)
    blocks = jnp.where(
        lax.rem(iota((1, ROWS), 1), REP) == plane, blocks_ref[...].astype(F32), 0.0
    )
    peer_block = nt(jnp.broadcast_to(blocks, (16, ROWS)).astype(BF16), repeat)[:1]
    hit = jnp.logical_and(
        peer_block == iota((128, 128), 0).astype(F32), iota((128, 128), 1) < SUB
    )
    by_block = hit.astype(F32)
    by_peer = jnp.transpose(by_block)
    mask = nn(by_block.astype(BF16), repeat).astype(BF16)
    mask_ref[...] = mask
    own_row = jnp.sum(
        jnp.where(iota((128, 128), 0) == own, by_peer, 0.0), axis=0, keepdims=True
    )
    own_ref[...] = jnp.broadcast_to(own_row, (8, 128))
    traces = ordered[CASES : CASES + 8]
    modes_ref[0] = traces
    own_part = jnp.concatenate(
        [row_sum(traces * traces[k : k + 1]) for k in range(MODES)], axis=0
    )

    @pl.loop(0, 4)
    def _(step):
        rows = pl.ds(pl.multiple_of(step * 256, 256), 256)
        half_ref[rows, :] = nn(operator_ref[0, rows, :], onehot_ref[...]).astype(BF16)

    exchange_wait(message, landed, send_a, receive_a, own, plane)
    partner = unpack(landed)
    residual = ordered[:CASES] - partner[:CASES]
    residual_ref[...] = residual
    far = partner[CASES : CASES + 8]
    modes_ref[1] = far
    pairs = jnp.concatenate([traces * far[k : k + 1] for k in range(MODES)], axis=0)
    crossed = 2.0 * (own_part * own_row - permuted(pairs, mask, nt))
    upright = jnp.transpose(jnp.concatenate([crossed, jnp.zeros((80, 128), F32)], axis=0))
    terms = [2.0 * row_sum(residual * traces[k : k + 1]) for k in range(MODES)]
    squares = row_sum(residual * residual)
    outgoing = upright[:AGGS]
    lane = iota((AGGS, 128), 1)
    for at, (upper, lower) in (
        (6, (terms[0], terms[1])),
        (30, (terms[2], terms[3])),
        (7, (terms[4], terms[5])),
        (31, (squares, jnp.zeros_like(squares))),
    ):
        outgoing = jnp.where(lane == at, jnp.concatenate([upper, lower], axis=0), outgoing)
    gram_out[...] = outgoing.reshape(AGGS, 1, 128)

    def give(i, _):
        peer = lax.rem(own + i, SUB)
        to_peer(
            gram_out.at[block_of(peer)], gram_in.at[own], send_b.at[peer], receive_b.at[own],
            peer, plane,
        ).start()
        return 0

    lax.fori_loop(1, SUB, give, 0)
    gram_in[own] = gram_out[block_of(own)]
    tall_route = jnp.transpose(jnp.broadcast_to(route_row, (128, ROWS)).astype(F32))
    for tile in range(8):
        hit = tall_route == (iota((ROWS, 128), 1) + tile * 128).astype(F32)
        rows_ref[:, tile * 128 : tile * 128 + 128] = hit.astype(F32).astype(BF16)
    exchange_wait(gram_out, gram_in, send_b, receive_b, own, plane)
    arrived = gram_in[...].reshape(SUB, 128)
    turned = jnp.transpose(jnp.concatenate([arrived, jnp.zeros((64, 128), F32)], axis=0))
    grouped = nn(turned[: 2 * HALF], by_peer, HIGHEST)
    part_ref[...] = grouped[:HALF] + pltpu.roll(grouped[HALF:], 64, 1)

    column(part_ref, column_in, send_c, receive_c, own, plane, "start")
    column_in[plane] = part_ref[...]

    @pl.loop(0, 4)
    def _(step):
        rows = pl.ds(pl.multiple_of(step * 256, 256), 256)
        glued_ref[rows, :] = nn(rows_ref[rows, :], half_ref[...]).astype(BF16)

    column(part_ref, column_in, send_c, receive_c, own, plane, "recv")
    total_ref[...] = jnp.sum(column_in[...], axis=0)

    line = own // 8
    group = lax.rem(own, 8)
    across = group // 2
    core = lax.rem(own, 2)

    def along_y(i, act):
        other = lax.rem(line + i, 8)
        index = group * 8 + (line if act == "start" else other)
        copy = to_peer(
            total_ref, gathered.at[index], send_d.at[other],
            receive_d.at[line if act == "start" else other], other * 8 + group, plane,
        )
        return copy

    def along_x(i, act):
        other = lax.rem(across + i, 4)
        source = gathered.at[pl.ds(8 * group, 8)]
        index = across if act == "start" else other
        return to_peer(
            source, gathered.at[pl.ds(8 * (2 * index + core), 8)], send_e.at[other],
            receive_e.at[index], line * 8 + 2 * other + core, plane,
        )

    def to_sibling(other, act):
        index = 2 * other + (core if act == "start" else 1 - core)
        return to_peer(
            gathered.at[pl.ds(8 * (2 * other + core), 8)], gathered.at[pl.ds(8 * index, 8)],
            send_f.at[other], receive_f.at[other], line * 8 + 2 * across + 1 - core, plane,
        )

    for i in range(1, 8):
        along_y(i, "start").start()
    gathered[block_of(own)] = total_ref[...]
    for i in range(1, 8):
        along_y(i, "recv").wait_recv()
    for i in range(1, 4):
        along_x(i, "start").start()
    to_sibling(across, "start").start()
    for i in (1, 3, 2):
        along_x(i, "recv").wait_recv()
        to_sibling(lax.rem(across + i, 4), "start").start()
    for i in range(4):
        to_sibling(i, "recv").wait_recv()

    low = iota((AGGS, 128), 1) < 64
    for k in range(3):
        for j in range(3):
            even = gathered[:, 8 * k + 2 * j, :]
            odd = gathered[:, 8 * k + 2 * j + 1, :]
            columns = pl.ds(128 * j, 128)
            gram_ref[64 * k : 64 * k + 64, columns] = jnp.where(low, even, pltpu.roll(odd, 64, 1))
            gram_ref[64 * k + 192 : 64 * k + 256, columns] = jnp.where(
                low, pltpu.roll(even, 64, 1), odd
            )
    near = gathered[:, 6, :]
    last = gathered[:, 7, :]
    folded = (near, pltpu.roll(near, 64, 1), last)
    for i in range(3):
        coarse_ref[:, 128 * i : 128 * i + 128] = jnp.where(
            low[:CASES], folded[i][:CASES], pltpu.roll(folded[i][CASES:], 64, 1)
        )
    norm_ref[...] = jnp.broadcast_to(
        row_sum(jnp.where(low[:CASES], 0.0, last[:CASES])), (CASES, 128)
    )
    exchange_sent(message, landed, send_a, receive_a, own, plane)
    exchange_sent(gram_out, gram_in, send_b, receive_b, own, plane)
    column(part_ref, column_in, send_c, receive_c, own, plane, "sent")
    for i in range(1, 8):
        along_y(i, "start").wait_send()
    for i in range(1, 4):
        along_x(i, "start").wait_send()
    for i in range(4):
        to_sibling(i, "start").wait_send()


def invert_block(pivot):
    tiles = pivot.reshape(16, 8, 128)
    lane = iota((8, 128), 1)
    line = iota((8, 128), 0)
    for k in range(0, 128, 4):
        tile, at = k // 8, k % 8
        lefts = [
            jnp.broadcast_to(tiles[:, :, k + m : k + m + 1], (16, 8, 128)) for m in range(4)
        ]
        rows = [
            jnp.broadcast_to(tiles[tile, at + m : at + m + 1, :], (8, 128)) for m in range(4)
        ]
        small = [
            [jnp.broadcast_to(lefts[n][tile, at + m : at + m + 1, :], (8, 128)) for n in range(4)]
            for m in range(4)
        ]
        for p in range(4):
            scale = 1.0 / small[p][p]
            pivots = [scale if n == p else small[p][n] * scale for n in range(4)]
            for m in range(4):
                if m != p:
                    factor = small[m][p]
                    small[m] = [
                        -factor * scale if n == p else small[m][n] - factor * pivots[n]
                        for n in range(4)
                    ]
            small[p] = pivots
        fresh = []
        for m in range(4):
            row = (small[m][0] * rows[0] + small[m][1] * rows[1]) + (
                small[m][2] * rows[2] + small[m][3] * rows[3]
            )
            for n in range(4):
                row = jnp.where(lane == k + n, small[m][n], row)
            fresh.append(row)
        inside = jnp.logical_and(lane >= k, lane < k + 4)
        kept = jnp.where(inside[None], 0.0, tiles)
        moved = kept - (
            (lefts[0] * fresh[0][None] + lefts[1] * fresh[1][None])
            + (lefts[2] * fresh[2][None] + lefts[3] * fresh[3][None])
        )
        own = moved[tile]
        for m in range(4):
            own = jnp.where(line == at + m, fresh[m], own)
        pieces = [own[None]]
        if tile > 0:
            pieces.insert(0, moved[:tile])
        if tile < 15:
            pieces.append(moved[tile + 1 :])
        tiles = jnp.concatenate(pieces, axis=0)
    return tiles.reshape(128, 128)


def invert_kernel(gram_ref, coarse_ref, parts_ref, start_ref, work):
    work[...] = gram_ref[...]

    @pl.loop(0, 3)
    def _(block):
        at = pl.ds(pl.multiple_of(block * 128, 128), 128)
        pivot = invert_block(work[at, at])
        rows = nn(pivot, work[at, :], HIGHEST)
        mine = iota((NC, 128), 0) // 128 == block
        lefts = jnp.where(mine, 0.0, work[:, at])
        work[...] = work[...] - nn(lefts, rows, HIGHEST)
        work[:, at] = -nn(lefts, pivot, HIGHEST)
        work[at, :] = rows
        work[at, at] = pivot

    high, middle, low = split(work[...])
    parts_ref[0] = high
    parts_ref[1] = middle
    parts_ref[2] = low
    start_ref[...] = solved(coarse_ref[...], parts_ref)


def solved(right, parts_ref):
    high, middle, low = split(right)
    one = nn(jnp.concatenate([high, middle, low], axis=0), parts_ref[0])
    two = nn(jnp.concatenate([high, middle], axis=0), parts_ref[1])
    three = nn(high, parts_ref[2])
    small = (one[2 * CASES :] + two[CASES:]) + three
    return one[:CASES] + ((one[CASES : 2 * CASES] + two[:CASES]) + small)


def coarse_terms(values, modes_ref, mask, own_row):
    far = jnp.concatenate([values * modes_ref[1, k : k + 1] for k in range(MODES)], axis=0)
    spread = permuted(far, mask, nt)
    columns = []
    for k in range(MODES):
        near = row_sum(values * modes_ref[0, k : k + 1])
        columns.append(2.0 * (near * own_row - spread[CASES * k : CASES * k + CASES]))
    return jnp.concatenate(
        [columns[2 * i] + pltpu.roll(columns[2 * i + 1], 64, 1) for i in range(3)], axis=1
    )


def expand(amounts, modes_ref, mask, own_row):
    low = iota((CASES, 128), 1) < 64
    pieces = []
    for i in range(3):
        both = amounts[:, 128 * i : 128 * i + 128]
        pieces.append(jnp.where(low, both, 0.0))
        pieces.append(jnp.where(low, pltpu.roll(both, 64, 1), 0.0))
    spread = permuted(jnp.concatenate(pieces, axis=0), mask, nn)
    total = None
    for k in range(MODES):
        near = row_sum(pieces[k] * own_row)
        term = near * modes_ref[0, k : k + 1] - spread[CASES * k : CASES * k + CASES] * modes_ref[1, k : k + 1]
        total = term if total is None else total + term
    return total


def owner_of(tile):
    return 4 * tile + lax.rem(tile, 4)


def reduce_start(pay, first_in, send, receive, own, plane):
    def one(tile, _):
        peer = owner_of(tile)

        @pl.when(peer != own)
        def _():
            to_peer(
                pay.at[tile], first_in.at[own], send.at[tile], receive.at[own], peer, plane
            ).start()

        return 0

    lax.fori_loop(0, TILES, one, 0)


def reduce_middle(pay, first_in, mid, second_in, last, result, sems, own, plane):
    send_1, receive_1, send_2, receive_2, send_3, receive_3 = sems
    tile = own // 4

    @pl.when(lax.rem(own, 4) == lax.rem(tile, 4))
    def _():
        first_in[own] = pay[tile]

        def one(i, _):
            peer = lax.rem(own + i, SUB)
            to_peer(
                pay.at[tile], first_in.at[peer], send_1.at[tile], receive_1.at[peer], peer, plane
            ).wait_recv()
            return 0

        lax.fori_loop(1, SUB, one, 0)
        mid[...] = jnp.sum(first_in[...], axis=0)
        column(mid, second_in, send_2, receive_2, own, plane, "start")
        second_in[plane] = mid[...]
        column(mid, second_in, send_2, receive_2, own, plane, "recv")
        last[...] = jnp.sum(second_in[...], axis=0)
        spread_start(last, result, tile, send_3, receive_3, own, plane)
        result[tile] = last[...]


def reduce_finish(pay, first_in, mid, second_in, last, result, sems, own, plane):
    send_1, receive_1, send_2, receive_2, send_3, receive_3 = sems

    def one(tile, _):
        peer = owner_of(tile)

        @pl.when(peer != own)
        def _():
            to_peer(
                last, result.at[tile], send_3.at[peer], receive_3.at[tile], peer, plane
            ).wait_recv()

        return 0

    lax.fori_loop(0, TILES, one, 0)


def reduce_sent(pay, first_in, mid, second_in, last, result, sems, own, plane):
    send_1, receive_1, send_2, receive_2, send_3, receive_3 = sems

    def one(tile, _):
        peer = owner_of(tile)

        @pl.when(peer != own)
        def _():
            to_peer(
                pay.at[tile], first_in.at[own], send_1.at[tile], receive_1.at[own], peer, plane
            ).wait_send()

        return 0

    lax.fori_loop(0, TILES, one, 0)
    tile = own // 4

    @pl.when(lax.rem(own, 4) == lax.rem(tile, 4))
    def _():
        column(mid, second_in, send_2, receive_2, own, plane, "sent")
        spread_sent(last, result, tile, send_3, receive_3, own, plane)


def load_pay(pay, sums, scalars):
    extra = jnp.zeros((CASES, 128), F32)
    for at, value in enumerate(scalars):
        extra = jnp.where(iota((CASES, 128), 1) == at, value, extra)
    for i in range(4):
        for j in range(3):
            pay[4 * i + j] = sums[8 * i : 8 * i + 8, 128 * j : 128 * j + 128]
        pay[4 * i + 3] = extra[8 * i : 8 * i + 8]


def read_result(result):
    columns = []
    for j in range(4):
        columns.append(jnp.concatenate([result[4 * i + j] for i in range(4)], axis=0))
    return jnp.concatenate(columns[:3], axis=1), columns[3]


def solve_kernel(
    residual_ref, modes_ref, mask_ref, own_ref, glued_ref, onehot_ref,
    parts_ref, start_ref, coarse_ref, norm_ref,
    multipliers_ref, amplitudes_ref,
    message, landed, pay_a, first_a, mid_a, second_a, last_a, result_a,
    pay_b, first_b, mid_b, second_b, last_b, result_b,
    send_x, receive_x,
    send_a1, receive_a1, send_a2, receive_a2, send_a3, receive_a3,
    send_b1, receive_b1, send_b2, receive_b2, send_b3, receive_b3,
):
    own = lax.axis_index("sub")
    plane = lax.axis_index("rep")
    barrier = greet(own, plane)
    round_a = (pay_a, first_a, mid_a, second_a, last_a, result_a,
               (send_a1, receive_a1, send_a2, receive_a2, send_a3, receive_a3), own, plane)
    round_b = (pay_b, first_b, mid_b, second_b, last_b, result_b,
               (send_b1, receive_b1, send_b2, receive_b2, send_b3, receive_b3), own, plane)

    residual = residual_ref[...]
    coarse = coarse_ref[...]
    start = start_ref[...]
    mask = mask_ref[...]
    own_row = own_ref[:1]
    direction = residual - expand(start, modes_ref, mask, own_row)
    inner = norm_ref[:, :1] - row_sum(start * coarse)
    product = nt(direction.astype(BF16), glued_ref[...])
    pack(jnp.concatenate([product, jnp.zeros((32, ROWS), F32)], axis=0), message)
    load_pay(
        pay_a,
        coarse_terms(product, modes_ref, mask, own_row),
        (2.0 * row_sum(direction * product),),
    )

    pl.semaphore_wait(barrier, SUB - 1 + REP - 1)
    reduce_start(pay_a, first_a, send_a1, receive_a1, own, plane)
    exchange_start(message, landed, send_x, receive_x, own, plane)
    flip_own(message, landed, own)
    reduce_middle(*round_a)
    exchange_wait(message, landed, send_x, receive_x, own, plane)
    jumped = product - unpack(landed)[:CASES]
    reduce_finish(*round_a)

    coarse_jump, sums = read_result(result_a)
    curvature = sums[:, 0:1]
    step = inner / curvature
    coarse_next = coarse - step * coarse_jump
    amplitudes = solved(coarse_next, parts_ref)
    projected = (residual - step * jumped) - expand(
        amplitudes, modes_ref, mask, own_row
    )
    high, low, _ = split(projected)
    both = nt(jnp.concatenate([high, low], axis=0), glued_ref[...])
    image = both[:CASES] + both[CASES:]
    load_pay(
        pay_b,
        coarse_terms(image, modes_ref, mask, own_row),
        (
            2.0 * row_sum(projected * image),
            2.0 * row_sum(projected * product) + 2.0 * row_sum(direction * image),
            row_sum(projected * projected),
        ),
    )
    reduce_start(pay_b, first_b, send_b1, receive_b1, own, plane)
    reduce_middle(*round_b)
    direction_rows = permuted(direction, onehot_ref[...], nt)
    projected_rows = permuted(projected, onehot_ref[...], nt)
    order = (
        iota((NC, NC), 1)
        == MODES * jnp.bitwise_and(iota((NC, NC), 0), AGGS - 1) + lax.shift_right_logical(iota((NC, NC), 0), 6)
    ).astype(F32).astype(BF16)
    exchange_sent(message, landed, send_x, receive_x, own, plane)
    reduce_sent(*round_a)
    reduce_finish(*round_b)

    image_coarse, sums = read_result(result_b)
    renewed = sums[:, 2:3]
    ratio = renewed / inner
    bend = sums[:, 0:1] + ratio * sums[:, 1:2] + ratio * ratio * curvature
    step_next = renewed / bend
    coarse_last = coarse_next - step_next * (image_coarse + ratio * coarse_jump)
    final = solved(coarse_last, parts_ref)
    amplitudes_ref[...] = permuted(final, order, nn)
    multipliers_ref[...] = (
        step * direction_rows + step_next * (projected_rows + ratio * direction_rows)
    )
    reduce_sent(*round_b)


VMEM = pl.BlockSpec(memory_space=pltpu.VMEM)
DMA = pltpu.SemaphoreType.DMA


def shape(dims, kind=F32):
    return jax.ShapeDtypeStruct(dims, kind)


def body(dual_ops, mode_traces, route, mode_block, local_gap):
    residual, modes, mask, own, glued, onehot, gram, coarse, norm = pl.pallas_call(
        setup_kernel,
        out_shape=(
            shape((CASES, ROWS)), shape((2, 8, ROWS)), shape((128, ROWS), BF16), shape((8, 128)),
            shape((ROWS, ROWS), BF16), shape((ROWS, ROWS), BF16),
            shape((NC, NC)), shape((CASES, NC)), shape((CASES, 128)),
        ),
        in_specs=[VMEM] * 5,
        out_specs=(VMEM,) * 9,
        scratch_shapes=[
            pltpu.VMEM((SUB, 8, 128), F32), pltpu.VMEM((SUB, 8, 128), F32),
            pltpu.VMEM((ROWS, ROWS), BF16), pltpu.VMEM((ROWS, ROWS), BF16),
            pltpu.VMEM((AGGS, 1, 128), F32), pltpu.VMEM((SUB, 1, 128), F32),
            pltpu.VMEM((SLICE, 128), F32), pltpu.VMEM((REP, SLICE, 128), F32),
            pltpu.VMEM((SLICE, 128), F32), pltpu.VMEM((AGGS, SLICE, 128), F32),
            DMA((SUB,)), DMA((SUB,)), DMA((SUB,)), DMA((SUB,)),
            DMA((REP,)), DMA((REP,)), DMA((8,)), DMA((8,)),
            DMA((4,)), DMA((4,)), DMA((4,)), DMA((4,)),
        ],
        compiler_params=pltpu.CompilerParams(
            collective_id=0, has_side_effects=True, vmem_limit_bytes=LIMIT
        ),
        name="setup",
    )(
        dual_ops,
        jnp.transpose(mode_traces, (1, 0, 2)),
        route,
        mode_block.reshape(1, SUB * REP),
        local_gap,
    )
    parts, start = pl.pallas_call(
        invert_kernel,
        out_shape=(shape((3, NC, NC), BF16), shape((CASES, NC))),
        in_specs=[VMEM] * 2,
        out_specs=(VMEM,) * 2,
        scratch_shapes=[pltpu.VMEM((NC, NC), F32)],
        compiler_params=pltpu.CompilerParams(vmem_limit_bytes=LIMIT),
        name="invert",
    )(gram, coarse)
    tile = pltpu.VMEM((8, 128), F32)
    many = pltpu.VMEM((SUB, 8, 128), F32)
    few = pltpu.VMEM((TILES, 8, 128), F32)
    return pl.pallas_call(
        solve_kernel,
        out_shape=(shape((CASES, ROWS)), shape((CASES, NC))),
        in_specs=[VMEM] * 10,
        out_specs=(VMEM,) * 2,
        scratch_shapes=[many, many] + [few, many, tile, few, tile, few] * 2
        + [DMA((SUB,)), DMA((SUB,))]
        + [DMA((TILES,)), DMA((SUB,)), DMA((REP,)), DMA((REP,)), DMA((SUB,)), DMA((TILES,))] * 2,
        compiler_params=pltpu.CompilerParams(
            collective_id=1, has_side_effects=True, vmem_limit_bytes=LIMIT
        ),
        name="solve",
    )(residual, modes, mask, own, glued, onehot, parts, start, coarse, norm)


def solution(mesh):
    placed = (
        P(("sub", "rep"), None, None),
        P(("sub", "rep"), None, None),
        P(("sub", "rep"), None),
        P(),
        P(None, ("sub", "rep")),
    )
    return jax.shard_map(
        body, mesh=mesh, in_specs=placed, out_specs=(P(None, ("sub", "rep")), P()), check_vma=False
    )
```

```python
import jax
import jax.numpy as jnp
from jax import lax
from jax.experimental import pallas as pl
from jax.experimental.pallas import tpu as pltpu
from jax.sharding import PartitionSpec as P

SUB = 64
REP = 16
PER = 16
ROWS = 1024
CASES = 32
MODES = 6
AGGS = 64
NC = 384
TILES = 16
SLICE = 24
HALF = 24
LIMIT = 24 * 1024 * 1024
F32 = jnp.float32
BF16 = jnp.bfloat16
HIGHEST = lax.Precision.HIGHEST
MESH = pl.DeviceIdType.MESH


def nt(left, right, precision=None):
    return lax.dot_general(
        left, right, (((1,), (1,)), ((), ())), precision=precision, preferred_element_type=F32
    )


def nn(left, right, precision=None):
    return lax.dot_general(
        left, right, (((1,), (0,)), ((), ())), precision=precision, preferred_element_type=F32
    )


def split(values):
    high = values.astype(BF16)
    rest = values - high.astype(F32)
    middle = rest.astype(BF16)
    low = (rest - middle.astype(F32)).astype(BF16)
    return high, middle, low


def stacked(values):
    return jnp.concatenate(split(values), axis=0)


def permuted(values, onehot, product):
    rows = values.shape[0]
    parts = product(stacked(values), onehot)
    return (parts[:rows] + parts[rows : 2 * rows]) + parts[2 * rows :]


def row_sum(values):
    return jnp.sum(values, axis=1, keepdims=True)


def iota(shape, dim):
    return lax.broadcasted_iota(jnp.int32, shape, dim)


def each_peer(act):
    def some(step, _):
        for j in range(7):
            act(lax.rem(step * 7 + (j + 23), SUB - 1) + 1)
        return 0

    lax.fori_loop(0, 9, some, 0)


def each_plane(act):
    def some(step, _):
        for j in range(5):
            act(lax.rem(step * 5 + (j + 5), REP - 1) + 1)
        return 0

    lax.fori_loop(0, 3, some, 0)


def greet(own, plane):
    barrier = pltpu.get_barrier_semaphore()

    def over_sub(i):
        pl.semaphore_signal(
            barrier, inc=1, device_id=(lax.rem(own + i, SUB), plane), device_id_type=MESH
        )

    def over_rep(i):
        pl.semaphore_signal(
            barrier, inc=1, device_id=(own, lax.rem(plane + i, REP)), device_id_type=MESH
        )

    each_plane(over_rep)
    each_peer(over_sub)
    return barrier


def to_peer(source, target, send, receive, peer, plane):
    return pltpu.make_async_remote_copy(
        src_ref=source,
        dst_ref=target,
        send_sem=send,
        recv_sem=receive,
        device_id=(peer, plane),
        device_id_type=MESH,
    )


def pack(values, message_ref):
    wide = jnp.concatenate([values, jnp.zeros((64, ROWS), F32)], axis=0)
    tall = jnp.transpose(wide).reshape(SUB, 2, 8, 128)
    message_ref[...] = tall[:, 0] + pltpu.roll(tall[:, 1], 64, 2)


def unpack(landed_ref):
    tiles = landed_ref[...]
    low = iota((SUB, 8, 128), 2) < 64
    first = jnp.where(low, tiles, 0.0)
    second = jnp.where(low, pltpu.roll(tiles, 64, 2), 0.0)
    tall = jnp.stack([first, second], axis=1).reshape(ROWS, 128)
    return jnp.transpose(tall)[:64]


def flip_own(message_ref, landed_ref, own):
    tile = pltpu.roll(message_ref[own], 64, 1)
    for a in range(8):
        landed_ref[own, pl.ds(7 - a, 1), :] = tile[a : a + 1, :]


def exchange_start(message_ref, landed_ref, send, receive, own, plane):
    def one(i):
        peer = lax.rem(own + i, SUB)
        to_peer(
            message_ref.at[peer], landed_ref.at[own], send.at[peer], receive.at[own], peer, plane
        ).start()

    each_peer(one)


def exchange_wait(message_ref, landed_ref, send, receive, own, plane):
    def one(i):
        peer = lax.rem(own + i, SUB)
        to_peer(
            message_ref.at[peer], landed_ref.at[peer], send.at[peer], receive.at[peer], peer, plane
        ).wait_recv()

    each_peer(one)


def exchange_sent(message_ref, landed_ref, send, receive, own, plane):
    def one(i):
        peer = lax.rem(own + i, SUB)
        to_peer(
            message_ref.at[peer], landed_ref.at[peer], send.at[peer], receive.at[peer], peer, plane
        ).wait_send()

    each_peer(one)


def spread_start(piece_ref, landed_ref, index, send, receive, own, plane):
    def one(i):
        peer = lax.rem(own + i, SUB)
        to_peer(
            piece_ref, landed_ref.at[index], send.at[peer], receive.at[index], peer, plane
        ).start()

    each_peer(one)


def spread_sent(piece_ref, landed_ref, index, send, receive, own, plane):
    def one(i):
        peer = lax.rem(own + i, SUB)
        to_peer(
            piece_ref, landed_ref.at[index], send.at[peer], receive.at[index], peer, plane
        ).wait_send()

    each_peer(one)


def column(piece_ref, landed_ref, send, receive, own, plane, act):
    def one(i):
        other = lax.rem(plane + i, REP)
        if act == "start":
            to_peer(
                piece_ref, landed_ref.at[plane], send.at[other], receive.at[plane], own, other
            ).start()
        elif act == "recv":
            to_peer(
                piece_ref, landed_ref.at[other], send.at[other], receive.at[other], own, other
            ).wait_recv()
        else:
            to_peer(
                piece_ref, landed_ref.at[other], send.at[other], receive.at[other], own, other
            ).wait_send()

    each_plane(one)


def block_of(peer):
    return lax.rem(peer, 8) * 8 + peer // 8


def setup_kernel(
    operator_in, traces_in, route_in, blocks_in, gap_in,
    residual_ref, modes_ref, mask_ref, own_ref, glued_ref, onehot_ref,
    gram_ref, coarse_ref, norm_ref,
    message, landed, rows_ref, half_ref,
    gram_out, gram_in, part_ref, column_in, total_ref, gathered,
    send_a, receive_a, send_b, receive_b, send_c, receive_c,
    send_d, receive_d, send_e, receive_e, send_f, receive_f,
    operator_ref, traces_ref, route_ref, blocks_ref, gap_ref, loaded,
):
    loads = [
        pltpu.make_async_copy(source, target, loaded.at[at])
        for at, (source, target) in enumerate((
            (route_in, route_ref), (gap_in, gap_ref), (traces_in, traces_ref),
            (blocks_in, blocks_ref), (operator_in, operator_ref),
        ))
    ]
    for load in loads:
        load.start()
    own = lax.axis_index("sub")
    plane = lax.axis_index("rep")
    barrier = greet(own, plane)

    loads[0].wait()
    route_row = route_ref[...]

    @pl.loop(0, 4)
    def _(step):
        rows = pl.ds(pl.multiple_of(step * 256, 256), 256)
        hit = iota((256, ROWS), 0) + step * 256 == route_row
        onehot_ref[rows, :] = hit.astype(F32).astype(BF16)

    loads[1].wait()
    loads[2].wait()
    natural = jnp.concatenate(
        [gap_ref[...]] + [traces_ref[k] for k in range(MODES)] + [jnp.zeros((10, ROWS), F32)],
        axis=0,
    )
    ordered = permuted(natural, onehot_ref[...], nn)
    pack(jnp.concatenate([ordered, jnp.zeros((16, ROWS), F32)], axis=0), message)

    pl.semaphore_wait(barrier, SUB - 1 + REP - 1)
    exchange_start(message, landed, send_a, receive_a, own, plane)
    flip_own(message, landed, own)

    loads[3].wait()
    loads[4].wait()
    repeat = (iota((128, ROWS), 1) // PER == iota((128, ROWS), 0)).astype(F32).astype(BF16)
    blocks = jnp.where(
        lax.rem(iota((1, ROWS), 1), REP) == plane, blocks_ref[...].astype(F32), 0.0
    )
    peer_block = nt(jnp.broadcast_to(blocks, (16, ROWS)).astype(BF16), repeat)[:1]
    hit = jnp.logical_and(
        peer_block == iota((128, 128), 0).astype(F32), iota((128, 128), 1) < SUB
    )
    by_block = hit.astype(F32)
    by_peer = jnp.transpose(by_block)
    mask = nn(by_block.astype(BF16), repeat).astype(BF16)
    mask_ref[...] = mask
    own_row = jnp.sum(
        jnp.where(iota((128, 128), 0) == own, by_peer, 0.0), axis=0, keepdims=True
    )
    own_ref[...] = jnp.broadcast_to(own_row, (8, 128))
    traces = ordered[CASES : CASES + 8]
    modes_ref[0] = traces
    own_part = jnp.concatenate(
        [row_sum(traces * traces[k : k + 1]) for k in range(MODES)], axis=0
    )

    @pl.loop(0, 4)
    def _(step):
        rows = pl.ds(pl.multiple_of(step * 256, 256), 256)
        half_ref[rows, :] = nn(operator_ref[0, rows, :], onehot_ref[...]).astype(BF16)

    exchange_wait(message, landed, send_a, receive_a, own, plane)
    partner = unpack(landed)
    residual = ordered[:CASES] - partner[:CASES]
    residual_ref[...] = residual
    far = partner[CASES : CASES + 8]
    modes_ref[1] = far
    pairs = jnp.concatenate([traces * far[k : k + 1] for k in range(MODES)], axis=0)
    crossed = 2.0 * (own_part * own_row - permuted(pairs, mask, nt))
    upright = jnp.transpose(jnp.concatenate([crossed, jnp.zeros((80, 128), F32)], axis=0))
    terms = [2.0 * row_sum(residual * traces[k : k + 1]) for k in range(MODES)]
    squares = row_sum(residual * residual)
    outgoing = upright[:AGGS]
    lane = iota((AGGS, 128), 1)
    for at, (upper, lower) in (
        (6, (terms[0], terms[1])),
        (30, (terms[2], terms[3])),
        (7, (terms[4], terms[5])),
        (31, (squares, jnp.zeros_like(squares))),
    ):
        outgoing = jnp.where(lane == at, jnp.concatenate([upper, lower], axis=0), outgoing)
    gram_out[...] = outgoing.reshape(AGGS, 1, 128)

    def give(i):
        peer = lax.rem(own + i, SUB)
        to_peer(
            gram_out.at[block_of(peer)], gram_in.at[own], send_b.at[peer], receive_b.at[own],
            peer, plane,
        ).start()

    each_peer(give)
    gram_in[own] = gram_out[block_of(own)]
    tall_route = jnp.transpose(jnp.broadcast_to(route_row, (128, ROWS)).astype(F32))
    for tile in range(8):
        hit = tall_route == (iota((ROWS, 128), 1) + tile * 128).astype(F32)
        rows_ref[:, tile * 128 : tile * 128 + 128] = hit.astype(F32).astype(BF16)
    exchange_wait(gram_out, gram_in, send_b, receive_b, own, plane)
    arrived = gram_in[...].reshape(SUB, 128)
    turned = jnp.transpose(jnp.concatenate([arrived, jnp.zeros((64, 128), F32)], axis=0))
    grouped = nn(turned[: 2 * HALF], by_peer, HIGHEST)
    part_ref[...] = grouped[:HALF] + pltpu.roll(grouped[HALF:], 64, 1)

    column(part_ref, column_in, send_c, receive_c, own, plane, "start")
    column_in[plane] = part_ref[...]

    @pl.loop(0, 4)
    def _(step):
        rows = pl.ds(pl.multiple_of(step * 256, 256), 256)
        glued_ref[rows, :] = nn(rows_ref[rows, :], half_ref[...]).astype(BF16)

    column(part_ref, column_in, send_c, receive_c, own, plane, "recv")
    total_ref[...] = jnp.sum(column_in[...], axis=0)

    line = own // 8
    group = lax.rem(own, 8)
    across = group // 2
    core = lax.rem(own, 2)

    def along_y(i, act):
        other = lax.rem(line + i, 8)
        index = group * 8 + (line if act == "start" else other)
        copy = to_peer(
            total_ref, gathered.at[index], send_d.at[other],
            receive_d.at[line if act == "start" else other], other * 8 + group, plane,
        )
        return copy

    def along_x(i, act):
        other = lax.rem(across + i, 4)
        source = gathered.at[pl.ds(8 * group, 8)]
        index = across if act == "start" else other
        return to_peer(
            source, gathered.at[pl.ds(8 * (2 * index + core), 8)], send_e.at[other],
            receive_e.at[index], line * 8 + 2 * other + core, plane,
        )

    def to_sibling(other, act):
        index = 2 * other + (core if act == "start" else 1 - core)
        return to_peer(
            gathered.at[pl.ds(8 * (2 * other + core), 8)], gathered.at[pl.ds(8 * index, 8)],
            send_f.at[other], receive_f.at[other], line * 8 + 2 * across + 1 - core, plane,
        )

    for i in range(1, 8):
        along_y(i, "start").start()
    gathered[block_of(own)] = total_ref[...]
    for i in range(1, 8):
        along_y(i, "recv").wait_recv()
    for i in range(1, 4):
        along_x(i, "start").start()
    to_sibling(across, "start").start()
    for i in (1, 3, 2):
        along_x(i, "recv").wait_recv()
        to_sibling(lax.rem(across + i, 4), "start").start()
    for i in range(4):
        to_sibling(i, "recv").wait_recv()

    low = iota((AGGS, 128), 1) < 64
    for k in range(3):
        for j in range(3):
            even = gathered[:, 8 * k + 2 * j, :]
            odd = gathered[:, 8 * k + 2 * j + 1, :]
            columns = pl.ds(128 * j, 128)
            gram_ref[64 * k : 64 * k + 64, columns] = jnp.where(low, even, pltpu.roll(odd, 64, 1))
            gram_ref[64 * k + 192 : 64 * k + 256, columns] = jnp.where(
                low, pltpu.roll(even, 64, 1), odd
            )
    near = gathered[:, 6, :]
    last = gathered[:, 7, :]
    folded = (near, pltpu.roll(near, 64, 1), last)
    for i in range(3):
        coarse_ref[:, 128 * i : 128 * i + 128] = jnp.where(
            low[:CASES], folded[i][:CASES], pltpu.roll(folded[i][CASES:], 64, 1)
        )
    norm_ref[...] = jnp.broadcast_to(
        row_sum(jnp.where(low[:CASES], 0.0, last[:CASES])), (CASES, 128)
    )
    exchange_sent(message, landed, send_a, receive_a, own, plane)
    exchange_sent(gram_out, gram_in, send_b, receive_b, own, plane)
    column(part_ref, column_in, send_c, receive_c, own, plane, "sent")
    for i in range(1, 8):
        along_y(i, "start").wait_send()
    for i in range(1, 4):
        along_x(i, "start").wait_send()
    for i in range(4):
        to_sibling(i, "start").wait_send()


def swapped(tiles, index, new):
    pieces = [new[None]]
    if index > 0:
        pieces.insert(0, tiles[:index])
    if index + 1 < tiles.shape[0]:
        pieces.append(tiles[index + 1 :])
    return jnp.concatenate(pieces, axis=0)


def invert_block(pivot):
    tiles = pivot.reshape(16, 8, 128)
    lane = iota((8, 128), 1)
    line = iota((8, 128), 0)
    for k in range(0, 128, 4):
        tile, at = k // 8, k % 8
        lefts = [
            jnp.broadcast_to(tiles[:, :, k + m : k + m + 1], (16, 8, 128)) for m in range(4)
        ]
        rows = [
            jnp.broadcast_to(tiles[tile, at + m : at + m + 1, :], (8, 128)) for m in range(4)
        ]
        small = [
            [jnp.broadcast_to(lefts[n][tile, at + m : at + m + 1, :], (8, 128)) for n in range(4)]
            for m in range(4)
        ]
        for p in range(4):
            scale = 1.0 / small[p][p]
            pivots = [scale if n == p else small[p][n] * scale for n in range(4)]
            for m in range(4):
                if m != p:
                    factor = small[m][p]
                    small[m] = [
                        -factor * scale if n == p else small[m][n] - factor * pivots[n]
                        for n in range(4)
                    ]
            small[p] = pivots
        inside = jnp.logical_and(lane >= k, lane < k + 4)
        ready = [
            jnp.where(inside, jnp.where(lane == k + m, 1.0, 0.0), rows[m]) for m in range(4)
        ]
        fresh = [
            (small[m][0] * ready[0] + small[m][1] * ready[1])
            + (small[m][2] * ready[2] + small[m][3] * ready[3])
            for m in range(4)
        ]
        chosen = jnp.logical_and(line >= at, line < at + 4)
        kept = jnp.where(inside[None], 0.0, tiles)
        kept = swapped(kept, tile, jnp.where(chosen, 0.0, kept[tile]))
        lefts = [
            swapped(
                lefts[m], tile,
                jnp.where(chosen, jnp.where(line == at + m, -1.0, 0.0), lefts[m][tile]),
            )
            for m in range(4)
        ]
        tiles = kept - (
            (lefts[0] * fresh[0][None] + lefts[1] * fresh[1][None])
            + (lefts[2] * fresh[2][None] + lefts[3] * fresh[3][None])
        )
    return tiles.reshape(128, 128)


def invert(gram_ref, parts_ref, work):
    work[...] = gram_ref[...]

    @pl.loop(0, 3)
    def _(block):
        at = pl.ds(pl.multiple_of(block * 128, 128), 128)
        pivot = invert_block(work[at, at])
        rows = nn(pivot, work[at, :], HIGHEST)
        mine = iota((NC, 128), 0) // 128 == block
        lefts = jnp.where(mine, 0.0, work[:, at])
        work[...] = work[...] - nn(lefts, rows, HIGHEST)
        work[:, at] = -nn(lefts, pivot, HIGHEST)
        work[at, :] = rows
        work[at, at] = pivot

    high, middle, low = split(work[...])
    parts_ref[0] = high
    parts_ref[1] = middle
    parts_ref[2] = low


def solved(right, parts_ref):
    high, middle, low = split(right)
    one = nn(jnp.concatenate([high, middle, low], axis=0), parts_ref[0])
    two = nn(jnp.concatenate([high, middle], axis=0), parts_ref[1])
    three = nn(high, parts_ref[2])
    small = (one[2 * CASES :] + two[CASES:]) + three
    return one[:CASES] + ((one[CASES : 2 * CASES] + two[:CASES]) + small)


def coarse_terms(values, modes_ref, mask, own_row):
    far = jnp.concatenate([values * modes_ref[1, k : k + 1] for k in range(MODES)], axis=0)
    spread = permuted(far, mask, nt)
    columns = []
    for k in range(MODES):
        near = row_sum(values * modes_ref[0, k : k + 1])
        columns.append(2.0 * (near * own_row - spread[CASES * k : CASES * k + CASES]))
    return jnp.concatenate(
        [columns[2 * i] + pltpu.roll(columns[2 * i + 1], 64, 1) for i in range(3)], axis=1
    )


def expand(amounts, modes_ref, mask, own_row):
    low = iota((CASES, 128), 1) < 64
    pieces = []
    for i in range(3):
        both = amounts[:, 128 * i : 128 * i + 128]
        pieces.append(jnp.where(low, both, 0.0))
        pieces.append(jnp.where(low, pltpu.roll(both, 64, 1), 0.0))
    spread = permuted(jnp.concatenate(pieces, axis=0), mask, nn)
    total = None
    for k in range(MODES):
        near = row_sum(pieces[k] * own_row)
        term = near * modes_ref[0, k : k + 1] - spread[CASES * k : CASES * k + CASES] * modes_ref[1, k : k + 1]
        total = term if total is None else total + term
    return total


def owner_of(tile):
    return 4 * tile + lax.rem(tile, 4)


def each_tile(act):
    def some(step, _):
        for j in range(4):
            act(step * 4 + j)
        return 0

    lax.fori_loop(0, 4, some, 0)


def reduce_start(pay, first_in, send, receive, own, plane):
    def one(tile):
        peer = owner_of(tile)

        @pl.when(peer != own)
        def _():
            to_peer(
                pay.at[tile], first_in.at[own], send.at[tile], receive.at[own], peer, plane
            ).start()

    each_tile(one)


def reduce_middle(pay, first_in, mid, second_in, last, result, sems, own, plane):
    send_1, receive_1, send_2, receive_2, send_3, receive_3 = sems
    tile = own // 4

    @pl.when(lax.rem(own, 4) == lax.rem(tile, 4))
    def _():
        first_in[own] = pay[tile]

        def one(i):
            peer = lax.rem(own + i, SUB)
            to_peer(
                pay.at[tile], first_in.at[peer], send_1.at[tile], receive_1.at[peer], peer, plane
            ).wait_recv()

        each_peer(one)
        mid[...] = jnp.sum(first_in[...], axis=0)
        column(mid, second_in, send_2, receive_2, own, plane, "start")
        second_in[plane] = mid[...]
        column(mid, second_in, send_2, receive_2, own, plane, "recv")
        last[...] = jnp.sum(second_in[...], axis=0)
        spread_start(last, result, tile, send_3, receive_3, own, plane)
        result[tile] = last[...]


def reduce_finish(pay, first_in, mid, second_in, last, result, sems, own, plane):
    send_1, receive_1, send_2, receive_2, send_3, receive_3 = sems

    def one(tile):
        peer = owner_of(tile)

        @pl.when(peer != own)
        def _():
            to_peer(
                last, result.at[tile], send_3.at[peer], receive_3.at[tile], peer, plane
            ).wait_recv()

    each_tile(one)


def reduce_sent(pay, first_in, mid, second_in, last, result, sems, own, plane):
    send_1, receive_1, send_2, receive_2, send_3, receive_3 = sems

    def one(tile):
        peer = owner_of(tile)

        @pl.when(peer != own)
        def _():
            to_peer(
                pay.at[tile], first_in.at[own], send_1.at[tile], receive_1.at[own], peer, plane
            ).wait_send()

    each_tile(one)
    tile = own // 4

    @pl.when(lax.rem(own, 4) == lax.rem(tile, 4))
    def _():
        column(mid, second_in, send_2, receive_2, own, plane, "sent")
        spread_sent(last, result, tile, send_3, receive_3, own, plane)


def load_pay(pay, sums, scalars):
    extra = jnp.zeros((CASES, 128), F32)
    for at, value in enumerate(scalars):
        extra = jnp.where(iota((CASES, 128), 1) == at, value, extra)
    for i in range(4):
        for j in range(3):
            pay[4 * i + j] = sums[8 * i : 8 * i + 8, 128 * j : 128 * j + 128]
        pay[4 * i + 3] = extra[8 * i : 8 * i + 8]


def read_result(result):
    columns = []
    for j in range(4):
        columns.append(jnp.concatenate([result[4 * i + j] for i in range(4)], axis=0))
    return jnp.concatenate(columns[:3], axis=1), columns[3]


def solve_kernel(
    residual_ref, modes_ref, mask_ref, own_ref, glued_ref, onehot_ref,
    gram_ref, coarse_ref, norm_ref,
    multipliers_ref, amplitudes_ref, parts_ref, work,
    message, landed, pay_a, first_a, mid_a, second_a, last_a, result_a,
    pay_b, first_b, mid_b, second_b, last_b, result_b,
    send_x, receive_x,
    send_a1, receive_a1, send_a2, receive_a2, send_a3, receive_a3,
    send_b1, receive_b1, send_b2, receive_b2, send_b3, receive_b3,
):
    own = lax.axis_index("sub")
    plane = lax.axis_index("rep")
    barrier = greet(own, plane)
    round_a = (pay_a, first_a, mid_a, second_a, last_a, result_a,
               (send_a1, receive_a1, send_a2, receive_a2, send_a3, receive_a3), own, plane)
    round_b = (pay_b, first_b, mid_b, second_b, last_b, result_b,
               (send_b1, receive_b1, send_b2, receive_b2, send_b3, receive_b3), own, plane)

    residual = residual_ref[...]
    coarse = coarse_ref[...]
    invert(gram_ref, parts_ref, work)
    start = solved(coarse, parts_ref)
    mask = mask_ref[...]
    own_row = own_ref[:1]
    direction = residual - expand(start, modes_ref, mask, own_row)
    inner = norm_ref[:, :1] - row_sum(start * coarse)
    product = nt(direction.astype(BF16), glued_ref[...])
    pack(jnp.concatenate([product, jnp.zeros((32, ROWS), F32)], axis=0), message)
    load_pay(
        pay_a,
        coarse_terms(product, modes_ref, mask, own_row),
        (2.0 * row_sum(direction * product),),
    )

    pl.semaphore_wait(barrier, SUB - 1 + REP - 1)
    reduce_start(pay_a, first_a, send_a1, receive_a1, own, plane)
    exchange_start(message, landed, send_x, receive_x, own, plane)
    flip_own(message, landed, own)
    reduce_middle(*round_a)
    exchange_wait(message, landed, send_x, receive_x, own, plane)
    jumped = product - unpack(landed)[:CASES]
    reduce_finish(*round_a)

    coarse_jump, sums = read_result(result_a)
    curvature = sums[:, 0:1]
    step = inner / curvature
    coarse_next = coarse - step * coarse_jump
    amplitudes = solved(coarse_next, parts_ref)
    projected = (residual - step * jumped) - expand(
        amplitudes, modes_ref, mask, own_row
    )
    high, low, _ = split(projected)
    both = nt(jnp.concatenate([high, low], axis=0), glued_ref[...])
    image = both[:CASES] + both[CASES:]
    load_pay(
        pay_b,
        coarse_terms(image, modes_ref, mask, own_row),
        (
            2.0 * row_sum(projected * image),
            2.0 * row_sum(projected * product) + 2.0 * row_sum(direction * image),
            row_sum(projected * projected),
        ),
    )
    reduce_start(pay_b, first_b, send_b1, receive_b1, own, plane)
    reduce_middle(*round_b)
    direction_rows = permuted(direction, onehot_ref[...], nt)
    projected_rows = permuted(projected, onehot_ref[...], nt)
    order = (
        iota((NC, NC), 1)
        == MODES * jnp.bitwise_and(iota((NC, NC), 0), AGGS - 1) + lax.shift_right_logical(iota((NC, NC), 0), 6)
    ).astype(F32).astype(BF16)
    exchange_sent(message, landed, send_x, receive_x, own, plane)
    reduce_sent(*round_a)
    reduce_finish(*round_b)

    image_coarse, sums = read_result(result_b)
    renewed = sums[:, 2:3]
    ratio = renewed / inner
    bend = sums[:, 0:1] + ratio * sums[:, 1:2] + ratio * ratio * curvature
    step_next = renewed / bend
    coarse_last = coarse_next - step_next * (image_coarse + ratio * coarse_jump)
    final = solved(coarse_last, parts_ref)
    amplitudes_ref[...] = permuted(final, order, nn)
    multipliers_ref[...] = (
        step * direction_rows + step_next * (projected_rows + ratio * direction_rows)
    )
    reduce_sent(*round_b)


VMEM = pl.BlockSpec(memory_space=pltpu.VMEM)
DMA = pltpu.SemaphoreType.DMA


def shape(dims, kind=F32):
    return jax.ShapeDtypeStruct(dims, kind)


def body(dual_ops, mode_traces, route, mode_block, local_gap):
    residual, modes, mask, own, glued, onehot, gram, coarse, norm = pl.pallas_call(
        setup_kernel,
        out_shape=(
            shape((CASES, ROWS)), shape((2, 8, ROWS)), shape((128, ROWS), BF16), shape((8, 128)),
            shape((ROWS, ROWS), BF16), shape((ROWS, ROWS), BF16),
            shape((NC, NC)), shape((CASES, NC)), shape((CASES, 128)),
        ),
        in_specs=[pl.BlockSpec(memory_space=pltpu.HBM)] * 5,
        out_specs=(VMEM,) * 9,
        scratch_shapes=[
            pltpu.VMEM((SUB, 8, 128), F32), pltpu.VMEM((SUB, 8, 128), F32),
            pltpu.VMEM((ROWS, ROWS), BF16), pltpu.VMEM((ROWS, ROWS), BF16),
            pltpu.VMEM((AGGS, 1, 128), F32), pltpu.VMEM((SUB, 1, 128), F32),
            pltpu.VMEM((SLICE, 128), F32), pltpu.VMEM((REP, SLICE, 128), F32),
            pltpu.VMEM((SLICE, 128), F32), pltpu.VMEM((AGGS, SLICE, 128), F32),
            DMA((SUB,)), DMA((SUB,)), DMA((SUB,)), DMA((SUB,)),
            DMA((REP,)), DMA((REP,)), DMA((8,)), DMA((8,)),
            DMA((4,)), DMA((4,)), DMA((4,)), DMA((4,)),
            pltpu.VMEM((1, ROWS, ROWS), BF16), pltpu.VMEM((MODES, 1, ROWS), F32),
            pltpu.VMEM((1, ROWS), jnp.int32), pltpu.VMEM((1, SUB * REP), jnp.int32),
            pltpu.VMEM((CASES, ROWS), F32), DMA((5,)),
        ],
        compiler_params=pltpu.CompilerParams(
            collective_id=0, has_side_effects=True, vmem_limit_bytes=LIMIT
        ),
        name="setup",
    )(
        dual_ops,
        jnp.transpose(mode_traces, (1, 0, 2)),
        route,
        mode_block.reshape(1, SUB * REP),
        local_gap,
    )
    tile = pltpu.VMEM((8, 128), F32)
    many = pltpu.VMEM((SUB, 8, 128), F32)
    few = pltpu.VMEM((TILES, 8, 128), F32)
    return pl.pallas_call(
        solve_kernel,
        out_shape=(shape((CASES, ROWS)), shape((CASES, NC))),
        in_specs=[VMEM] * 9,
        out_specs=(VMEM,) * 2,
        scratch_shapes=[pltpu.VMEM((3, NC, NC), BF16), pltpu.VMEM((NC, NC), F32), many, many] + [few, many, tile, few, tile, few] * 2
        + [DMA((SUB,)), DMA((SUB,))]
        + [DMA((TILES,)), DMA((SUB,)), DMA((REP,)), DMA((REP,)), DMA((SUB,)), DMA((TILES,))] * 2,
        compiler_params=pltpu.CompilerParams(
            collective_id=1, has_side_effects=True, vmem_limit_bytes=LIMIT
        ),
        name="solve",
    )(residual, modes, mask, own, glued, onehot, gram, coarse, norm)


def solution(mesh):
    placed = (
        P(("sub", "rep"), None, None),
        P(("sub", "rep"), None, None),
        P(("sub", "rep"), None),
        P(),
        P(None, ("sub", "rep")),
    )
    return jax.shard_map(
        body, mesh=mesh, in_specs=placed, out_specs=(P(None, ("sub", "rep")), P()), check_vma=False
    )
```

```python
import jax
import jax.numpy as jnp
from jax import lax
from jax.experimental import pallas as pl
from jax.experimental.pallas import tpu as pltpu
from jax.sharding import PartitionSpec as P

SUB = 64
REP = 16
PER = 16
ROWS = 1024
CASES = 32
MODES = 6
AGGS = 64
NC = 384
TILES = 16
SLICE = 24
HALF = 24
LIMIT = 60 * 1024 * 1024
F32 = jnp.float32
BF16 = jnp.bfloat16
HIGHEST = lax.Precision.HIGHEST
MESH = pl.DeviceIdType.MESH


def nt(left, right, precision=None):
    return lax.dot_general(
        left, right, (((1,), (1,)), ((), ())), precision=precision, preferred_element_type=F32
    )


def nn(left, right, precision=None):
    return lax.dot_general(
        left, right, (((1,), (0,)), ((), ())), precision=precision, preferred_element_type=F32
    )


def split(values):
    high = values.astype(BF16)
    rest = values - high.astype(F32)
    middle = rest.astype(BF16)
    low = (rest - middle.astype(F32)).astype(BF16)
    return high, middle, low


def stacked(values):
    return jnp.concatenate(split(values), axis=0)


def permuted(values, onehot, product):
    rows = values.shape[0]
    parts = product(stacked(values), onehot)
    return (parts[:rows] + parts[rows : 2 * rows]) + parts[2 * rows :]


def row_sum(values):
    return jnp.sum(values, axis=1, keepdims=True)


def iota(shape, dim):
    return lax.broadcasted_iota(jnp.int32, shape, dim)


def each_peer(act):
    def some(step, _):
        for j in range(7):
            act(lax.rem(step * 7 + (j + 23), SUB - 1) + 1)
        return 0

    lax.fori_loop(0, 9, some, 0)


def each_plane(act):
    def some(step, _):
        for j in range(5):
            act(lax.rem(step * 5 + (j + 5), REP - 1) + 1)
        return 0

    lax.fori_loop(0, 3, some, 0)


def greet(own, plane):
    barrier = pltpu.get_barrier_semaphore()

    def over_sub(i):
        pl.semaphore_signal(
            barrier, inc=1, device_id=(lax.rem(own + i, SUB), plane), device_id_type=MESH
        )

    def over_rep(i):
        pl.semaphore_signal(
            barrier, inc=1, device_id=(own, lax.rem(plane + i, REP)), device_id_type=MESH
        )

    each_plane(over_rep)
    each_peer(over_sub)
    return barrier


def to_peer(source, target, send, receive, peer, plane):
    return pltpu.make_async_remote_copy(
        src_ref=source,
        dst_ref=target,
        send_sem=send,
        recv_sem=receive,
        device_id=(peer, plane),
        device_id_type=MESH,
    )


def pack(values, message_ref):
    wide = jnp.concatenate([values, jnp.zeros((64, ROWS), F32)], axis=0)
    tall = jnp.transpose(wide).reshape(SUB, 2, 8, 128)
    message_ref[...] = tall[:, 0] + pltpu.roll(tall[:, 1], 64, 2)


def unpack(landed_ref):
    tiles = landed_ref[...]
    low = iota((SUB, 8, 128), 2) < 64
    first = jnp.where(low, tiles, 0.0)
    second = jnp.where(low, pltpu.roll(tiles, 64, 2), 0.0)
    tall = jnp.stack([first, second], axis=1).reshape(ROWS, 128)
    return jnp.transpose(tall)[:64]


def flip_own(message_ref, landed_ref, own):
    tile = pltpu.roll(message_ref[own], 64, 1)
    for a in range(8):
        landed_ref[own, pl.ds(7 - a, 1), :] = tile[a : a + 1, :]


def exchange_start(message_ref, landed_ref, send, receive, own, plane):
    def one(i):
        peer = lax.rem(own + i, SUB)
        to_peer(
            message_ref.at[peer], landed_ref.at[own], send.at[peer], receive.at[own], peer, plane
        ).start()

    each_peer(one)


def exchange_wait(message_ref, landed_ref, send, receive, own, plane):
    def one(i):
        peer = lax.rem(own + i, SUB)
        to_peer(
            message_ref.at[peer], landed_ref.at[peer], send.at[peer], receive.at[peer], peer, plane
        ).wait_recv()

    each_peer(one)


def exchange_sent(message_ref, landed_ref, send, receive, own, plane):
    def one(i):
        peer = lax.rem(own + i, SUB)
        to_peer(
            message_ref.at[peer], landed_ref.at[peer], send.at[peer], receive.at[peer], peer, plane
        ).wait_send()

    each_peer(one)


def spread_start(piece_ref, landed_ref, index, send, receive, own, plane):
    def one(i):
        peer = lax.rem(own + i, SUB)
        to_peer(
            piece_ref, landed_ref.at[index], send.at[peer], receive.at[index], peer, plane
        ).start()

    each_peer(one)


def spread_sent(piece_ref, landed_ref, index, send, receive, own, plane):
    def one(i):
        peer = lax.rem(own + i, SUB)
        to_peer(
            piece_ref, landed_ref.at[index], send.at[peer], receive.at[index], peer, plane
        ).wait_send()

    each_peer(one)


def column(piece_ref, landed_ref, send, receive, own, plane, act):
    def one(i):
        other = lax.rem(plane + i, REP)
        if act == "start":
            to_peer(
                piece_ref, landed_ref.at[plane], send.at[other], receive.at[plane], own, other
            ).start()
        elif act == "recv":
            to_peer(
                piece_ref, landed_ref.at[other], send.at[other], receive.at[other], own, other
            ).wait_recv()
        else:
            to_peer(
                piece_ref, landed_ref.at[other], send.at[other], receive.at[other], own, other
            ).wait_send()

    each_plane(one)


def block_of(peer):
    return lax.rem(peer, 8) * 8 + peer // 8


def setup_kernel(
    operator_in, traces_in, route_in, blocks_in, gap_in,
    residual_ref, modes_ref, mask_ref, own_ref, glued_ref, onehot_ref,
    gram_ref, coarse_ref, norm_ref,
    message, landed, rows_ref, half_ref,
    gram_out, gram_in, part_ref, column_in, total_ref, gathered,
    send_a, receive_a, send_b, receive_b, send_c, receive_c,
    send_d, receive_d, send_e, receive_e, send_f, receive_f,
    operator_ref, traces_ref, route_ref, blocks_ref, gap_ref, loaded,
):
    loads = [
        pltpu.make_async_copy(source, target, loaded.at[at])
        for at, (source, target) in enumerate((
            (route_in, route_ref), (gap_in, gap_ref), (traces_in, traces_ref),
            (blocks_in, blocks_ref), (operator_in, operator_ref),
        ))
    ]
    for load in loads:
        load.start()
    own = lax.axis_index("sub")
    plane = lax.axis_index("rep")
    barrier = greet(own, plane)

    loads[0].wait()
    route_row = route_ref[...]

    @pl.loop(0, 4)
    def _(step):
        rows = pl.ds(pl.multiple_of(step * 256, 256), 256)
        hit = iota((256, ROWS), 0) + step * 256 == route_row
        onehot_ref[rows, :] = hit.astype(F32).astype(BF16)

    loads[1].wait()
    loads[2].wait()
    natural = jnp.concatenate(
        [gap_ref[...]] + [traces_ref[k] for k in range(MODES)] + [jnp.zeros((10, ROWS), F32)],
        axis=0,
    )
    ordered = permuted(natural, onehot_ref[...], nn)
    pack(jnp.concatenate([ordered, jnp.zeros((16, ROWS), F32)], axis=0), message)

    pl.semaphore_wait(barrier, SUB - 1 + REP - 1)
    exchange_start(message, landed, send_a, receive_a, own, plane)
    flip_own(message, landed, own)

    loads[3].wait()
    loads[4].wait()
    repeat = (iota((128, ROWS), 1) // PER == iota((128, ROWS), 0)).astype(F32).astype(BF16)
    blocks = jnp.where(
        lax.rem(iota((1, ROWS), 1), REP) == plane, blocks_ref[...].astype(F32), 0.0
    )
    peer_block = nt(jnp.broadcast_to(blocks, (16, ROWS)).astype(BF16), repeat)[:1]
    hit = jnp.logical_and(
        peer_block == iota((128, 128), 0).astype(F32), iota((128, 128), 1) < SUB
    )
    by_block = hit.astype(F32)
    by_peer = jnp.transpose(by_block)
    mask = nn(by_block.astype(BF16), repeat).astype(BF16)
    mask_ref[...] = mask
    own_row = jnp.sum(
        jnp.where(iota((128, 128), 0) == own, by_peer, 0.0), axis=0, keepdims=True
    )
    own_ref[...] = jnp.broadcast_to(own_row, (8, 128))
    traces = ordered[CASES : CASES + 8]
    modes_ref[0] = traces
    own_part = jnp.concatenate(
        [row_sum(traces * traces[k : k + 1]) for k in range(MODES)], axis=0
    )

    @pl.loop(0, 4)
    def _(step):
        rows = pl.ds(pl.multiple_of(step * 256, 256), 256)
        half_ref[rows, :] = nn(operator_ref[0, rows, :], onehot_ref[...]).astype(BF16)

    exchange_wait(message, landed, send_a, receive_a, own, plane)
    partner = unpack(landed)
    residual = ordered[:CASES] - partner[:CASES]
    residual_ref[...] = residual
    far = partner[CASES : CASES + 8]
    modes_ref[1] = far
    pairs = jnp.concatenate([traces * far[k : k + 1] for k in range(MODES)], axis=0)
    crossed = 2.0 * (own_part * own_row - permuted(pairs, mask, nt))
    upright = jnp.transpose(jnp.concatenate([crossed, jnp.zeros((80, 128), F32)], axis=0))
    terms = [2.0 * row_sum(residual * traces[k : k + 1]) for k in range(MODES)]
    squares = row_sum(residual * residual)
    outgoing = upright[:AGGS]
    lane = iota((AGGS, 128), 1)
    for at, (upper, lower) in (
        (6, (terms[0], terms[1])),
        (30, (terms[2], terms[3])),
        (7, (terms[4], terms[5])),
        (31, (squares, jnp.zeros_like(squares))),
    ):
        outgoing = jnp.where(lane == at, jnp.concatenate([upper, lower], axis=0), outgoing)
    gram_out[...] = outgoing.reshape(AGGS, 1, 128)

    def give(i):
        peer = lax.rem(own + i, SUB)
        to_peer(
            gram_out.at[block_of(peer)], gram_in.at[own], send_b.at[peer], receive_b.at[own],
            peer, plane,
        ).start()

    each_peer(give)
    gram_in[own] = gram_out[block_of(own)]
    tall_route = jnp.transpose(jnp.broadcast_to(route_row, (128, ROWS)).astype(F32))
    for tile in range(8):
        hit = tall_route == (iota((ROWS, 128), 1) + tile * 128).astype(F32)
        rows_ref[:, tile * 128 : tile * 128 + 128] = hit.astype(F32).astype(BF16)
    exchange_wait(gram_out, gram_in, send_b, receive_b, own, plane)
    arrived = gram_in[...].reshape(SUB, 128)
    turned = jnp.transpose(jnp.concatenate([arrived, jnp.zeros((64, 128), F32)], axis=0))
    grouped = nn(turned[: 2 * HALF], by_peer, HIGHEST)
    part_ref[...] = grouped[:HALF] + pltpu.roll(grouped[HALF:], 64, 1)

    column(part_ref, column_in, send_c, receive_c, own, plane, "start")
    column_in[plane] = part_ref[...]

    @pl.loop(0, 4)
    def _(step):
        rows = pl.ds(pl.multiple_of(step * 256, 256), 256)
        glued_ref[rows, :] = nn(rows_ref[rows, :], half_ref[...]).astype(BF16)

    column(part_ref, column_in, send_c, receive_c, own, plane, "recv")
    total_ref[...] = jnp.sum(column_in[...], axis=0)

    line = own // 8
    group = lax.rem(own, 8)
    across = group // 2
    core = lax.rem(own, 2)

    def along_y(i, act):
        other = lax.rem(line + i, 8)
        index = group * 8 + (line if act == "start" else other)
        copy = to_peer(
            total_ref, gathered.at[index], send_d.at[other],
            receive_d.at[line if act == "start" else other], other * 8 + group, plane,
        )
        return copy

    def along_x(i, act):
        other = lax.rem(across + i, 4)
        source = gathered.at[pl.ds(8 * group, 8)]
        index = across if act == "start" else other
        return to_peer(
            source, gathered.at[pl.ds(8 * (2 * index + core), 8)], send_e.at[other],
            receive_e.at[index], line * 8 + 2 * other + core, plane,
        )

    def to_sibling(other, act):
        index = 2 * other + (core if act == "start" else 1 - core)
        return to_peer(
            gathered.at[pl.ds(8 * (2 * other + core), 8)], gathered.at[pl.ds(8 * index, 8)],
            send_f.at[other], receive_f.at[other], line * 8 + 2 * across + 1 - core, plane,
        )

    for i in range(1, 8):
        along_y(i, "start").start()
    gathered[block_of(own)] = total_ref[...]
    for i in range(1, 8):
        along_y(i, "recv").wait_recv()
    for i in range(1, 4):
        along_x(i, "start").start()
    to_sibling(across, "start").start()
    for i in (1, 3, 2):
        along_x(i, "recv").wait_recv()
        to_sibling(lax.rem(across + i, 4), "start").start()
    for i in range(4):
        to_sibling(i, "recv").wait_recv()

    low = iota((AGGS, 128), 1) < 64
    for k in range(3):
        for j in range(3):
            even = gathered[:, 8 * k + 2 * j, :]
            odd = gathered[:, 8 * k + 2 * j + 1, :]
            columns = pl.ds(128 * j, 128)
            gram_ref[64 * k : 64 * k + 64, columns] = jnp.where(low, even, pltpu.roll(odd, 64, 1))
            gram_ref[64 * k + 192 : 64 * k + 256, columns] = jnp.where(
                low, pltpu.roll(even, 64, 1), odd
            )
    near = gathered[:, 6, :]
    last = gathered[:, 7, :]
    folded = (near, pltpu.roll(near, 64, 1), last)
    for i in range(3):
        coarse_ref[:, 128 * i : 128 * i + 128] = jnp.where(
            low[:CASES], folded[i][:CASES], pltpu.roll(folded[i][CASES:], 64, 1)
        )
    norm_ref[...] = jnp.broadcast_to(
        row_sum(jnp.where(low[:CASES], 0.0, last[:CASES])), (CASES, 128)
    )
    exchange_sent(message, landed, send_a, receive_a, own, plane)
    exchange_sent(gram_out, gram_in, send_b, receive_b, own, plane)
    column(part_ref, column_in, send_c, receive_c, own, plane, "sent")
    for i in range(1, 8):
        along_y(i, "start").wait_send()
    for i in range(1, 4):
        along_x(i, "start").wait_send()
    for i in range(4):
        to_sibling(i, "start").wait_send()


def swapped(tiles, index, new):
    pieces = [new[None]]
    if index > 0:
        pieces.insert(0, tiles[:index])
    if index + 1 < tiles.shape[0]:
        pieces.append(tiles[index + 1 :])
    return jnp.concatenate(pieces, axis=0)


def picked(values, chosen):
    return jnp.broadcast_to(
        jnp.sum(jnp.where(chosen, values, 0.0), axis=0, keepdims=True), (8, 128)
    )


def invert_block(pivot):
    tiles = pivot.reshape(16, 8, 128)
    lane = iota((8, 128), 1)
    line = iota((8, 128), 0)
    for k in range(0, 128, 4):
        tile, at = k // 8, k % 8
        lefts = [
            jnp.broadcast_to(tiles[:, :, k + m : k + m + 1], (16, 8, 128)) for m in range(4)
        ]
        rows = [
            jnp.broadcast_to(tiles[tile, at + m : at + m + 1, :], (8, 128)) for m in range(4)
        ]
        small = [
            [picked(lefts[n][tile], line == at + m) for n in range(4)]
            for m in range(4)
        ]
        for p in range(4):
            scale = 1.0 / small[p][p]
            pivots = [scale if n == p else small[p][n] * scale for n in range(4)]
            for m in range(4):
                if m != p:
                    factor = small[m][p]
                    small[m] = [
                        -factor * scale if n == p else small[m][n] - factor * pivots[n]
                        for n in range(4)
                    ]
            small[p] = pivots
        inside = jnp.logical_and(lane >= k, lane < k + 4)
        ready = [
            jnp.where(inside, jnp.where(lane == k + m, 1.0, 0.0), rows[m]) for m in range(4)
        ]
        fresh = [
            (small[m][0] * ready[0] + small[m][1] * ready[1])
            + (small[m][2] * ready[2] + small[m][3] * ready[3])
            for m in range(4)
        ]
        chosen = jnp.logical_and(line >= at, line < at + 4)
        kept = jnp.where(inside[None], 0.0, tiles)
        kept = swapped(kept, tile, jnp.where(chosen, 0.0, kept[tile]))
        lefts = [
            swapped(
                lefts[m], tile,
                jnp.where(chosen, jnp.where(line == at + m, -1.0, 0.0), lefts[m][tile]),
            )
            for m in range(4)
        ]
        tiles = kept - (
            (lefts[0] * fresh[0][None] + lefts[1] * fresh[1][None])
            + (lefts[2] * fresh[2][None] + lefts[3] * fresh[3][None])
        )
    return tiles.reshape(128, 128)


def invert(gram_ref, parts_ref, work):
    work[...] = gram_ref[...]

    @pl.loop(0, 3)
    def _(block):
        at = pl.ds(pl.multiple_of(block * 128, 128), 128)
        pivot = invert_block(work[at, at])
        rows = nn(pivot, work[at, :], HIGHEST)
        mine = iota((NC, 128), 0) // 128 == block
        lefts = jnp.where(mine, 0.0, work[:, at])
        work[...] = work[...] - nn(lefts, rows, HIGHEST)
        work[:, at] = -nn(lefts, pivot, HIGHEST)
        work[at, :] = rows
        work[at, at] = pivot

    high, middle, low = split(work[...])
    parts_ref[0] = high
    parts_ref[1] = middle
    parts_ref[2] = low


def solved(right, parts_ref):
    high, middle, low = split(right)
    one = nn(jnp.concatenate([high, middle, low], axis=0), parts_ref[0])
    two = nn(jnp.concatenate([high, middle], axis=0), parts_ref[1])
    three = nn(high, parts_ref[2])
    small = (one[2 * CASES :] + two[CASES:]) + three
    return one[:CASES] + ((one[CASES : 2 * CASES] + two[:CASES]) + small)


def coarse_terms(values, modes_ref, mask, own_row):
    far = jnp.concatenate([values * modes_ref[1, k : k + 1] for k in range(MODES)], axis=0)
    spread = permuted(far, mask, nt)
    columns = []
    for k in range(MODES):
        near = row_sum(values * modes_ref[0, k : k + 1])
        columns.append(2.0 * (near * own_row - spread[CASES * k : CASES * k + CASES]))
    return jnp.concatenate(
        [columns[2 * i] + pltpu.roll(columns[2 * i + 1], 64, 1) for i in range(3)], axis=1
    )


def expand(amounts, modes_ref, mask, own_row):
    low = iota((CASES, 128), 1) < 64
    pieces = []
    for i in range(3):
        both = amounts[:, 128 * i : 128 * i + 128]
        pieces.append(jnp.where(low, both, 0.0))
        pieces.append(jnp.where(low, pltpu.roll(both, 64, 1), 0.0))
    spread = permuted(jnp.concatenate(pieces, axis=0), mask, nn)
    total = None
    for k in range(MODES):
        near = row_sum(pieces[k] * own_row)
        term = near * modes_ref[0, k : k + 1] - spread[CASES * k : CASES * k + CASES] * modes_ref[1, k : k + 1]
        total = term if total is None else total + term
    return total


def owner_of(tile):
    return 4 * tile + lax.rem(tile, 4)


def each_tile(act):
    def some(step, _):
        for j in range(4):
            act(step * 4 + j)
        return 0

    lax.fori_loop(0, 4, some, 0)


def reduce_start(pay, first_in, send, receive, own, plane):
    def one(tile):
        peer = owner_of(tile)

        @pl.when(peer != own)
        def _():
            to_peer(
                pay.at[tile], first_in.at[own], send.at[tile], receive.at[own], peer, plane
            ).start()

    each_tile(one)


def reduce_middle(pay, first_in, mid, second_in, last, result, sems, own, plane):
    send_1, receive_1, send_2, receive_2, send_3, receive_3 = sems
    tile = own // 4

    @pl.when(lax.rem(own, 4) == lax.rem(tile, 4))
    def _():
        first_in[own] = pay[tile]

        def one(i):
            peer = lax.rem(own + i, SUB)
            to_peer(
                pay.at[tile], first_in.at[peer], send_1.at[tile], receive_1.at[peer], peer, plane
            ).wait_recv()

        each_peer(one)
        mid[...] = jnp.sum(first_in[...], axis=0)
        column(mid, second_in, send_2, receive_2, own, plane, "start")
        second_in[plane] = mid[...]
        column(mid, second_in, send_2, receive_2, own, plane, "recv")
        last[...] = jnp.sum(second_in[...], axis=0)
        spread_start(last, result, tile, send_3, receive_3, own, plane)
        result[tile] = last[...]


def reduce_finish(pay, first_in, mid, second_in, last, result, sems, own, plane):
    send_1, receive_1, send_2, receive_2, send_3, receive_3 = sems

    def one(tile):
        peer = owner_of(tile)

        @pl.when(peer != own)
        def _():
            to_peer(
                last, result.at[tile], send_3.at[peer], receive_3.at[tile], peer, plane
            ).wait_recv()

    each_tile(one)


def reduce_sent(pay, first_in, mid, second_in, last, result, sems, own, plane):
    send_1, receive_1, send_2, receive_2, send_3, receive_3 = sems

    def one(tile):
        peer = owner_of(tile)

        @pl.when(peer != own)
        def _():
            to_peer(
                pay.at[tile], first_in.at[own], send_1.at[tile], receive_1.at[own], peer, plane
            ).wait_send()

    each_tile(one)
    tile = own // 4

    @pl.when(lax.rem(own, 4) == lax.rem(tile, 4))
    def _():
        column(mid, second_in, send_2, receive_2, own, plane, "sent")
        spread_sent(last, result, tile, send_3, receive_3, own, plane)


def load_pay(pay, sums, scalars):
    extra = jnp.zeros((CASES, 128), F32)
    for at, value in enumerate(scalars):
        extra = jnp.where(iota((CASES, 128), 1) == at, value, extra)
    for i in range(4):
        for j in range(3):
            pay[4 * i + j] = sums[8 * i : 8 * i + 8, 128 * j : 128 * j + 128]
        pay[4 * i + 3] = extra[8 * i : 8 * i + 8]


def read_result(result):
    columns = []
    for j in range(4):
        columns.append(jnp.concatenate([result[4 * i + j] for i in range(4)], axis=0))
    return jnp.concatenate(columns[:3], axis=1), columns[3]


def solve_kernel(
    residual_ref, modes_ref, mask_ref, own_ref, glued_ref, onehot_ref,
    gram_ref, coarse_ref, norm_ref,
    multipliers_ref, amplitudes_ref, parts_ref, work,
    message, landed, pay_a, first_a, mid_a, second_a, last_a, result_a,
    pay_b, first_b, mid_b, second_b, last_b, result_b,
    send_x, receive_x,
    send_a1, receive_a1, send_a2, receive_a2, send_a3, receive_a3,
    send_b1, receive_b1, send_b2, receive_b2, send_b3, receive_b3,
):
    own = lax.axis_index("sub")
    plane = lax.axis_index("rep")
    round_a = (pay_a, first_a, mid_a, second_a, last_a, result_a,
               (send_a1, receive_a1, send_a2, receive_a2, send_a3, receive_a3), own, plane)
    round_b = (pay_b, first_b, mid_b, second_b, last_b, result_b,
               (send_b1, receive_b1, send_b2, receive_b2, send_b3, receive_b3), own, plane)

    residual = residual_ref[...]
    coarse = coarse_ref[...]
    invert(gram_ref, parts_ref, work)
    start = solved(coarse, parts_ref)
    mask = mask_ref[...]
    own_row = own_ref[:1]
    direction = residual - expand(start, modes_ref, mask, own_row)
    inner = norm_ref[:, :1] - row_sum(start * coarse)
    product = nt(direction.astype(BF16), glued_ref[...])
    pack(jnp.concatenate([product, jnp.zeros((32, ROWS), F32)], axis=0), message)
    load_pay(
        pay_a,
        coarse_terms(product, modes_ref, mask, own_row),
        (2.0 * row_sum(direction * product),),
    )

    reduce_start(pay_a, first_a, send_a1, receive_a1, own, plane)
    exchange_start(message, landed, send_x, receive_x, own, plane)
    flip_own(message, landed, own)
    reduce_middle(*round_a)
    exchange_wait(message, landed, send_x, receive_x, own, plane)
    jumped = product - unpack(landed)[:CASES]
    reduce_finish(*round_a)

    coarse_jump, sums = read_result(result_a)
    curvature = sums[:, 0:1]
    step = inner / curvature
    coarse_next = coarse - step * coarse_jump
    amplitudes = solved(coarse_next, parts_ref)
    projected = (residual - step * jumped) - expand(
        amplitudes, modes_ref, mask, own_row
    )
    high, low, _ = split(projected)
    both = nt(jnp.concatenate([high, low], axis=0), glued_ref[...])
    image = both[:CASES] + both[CASES:]
    load_pay(
        pay_b,
        coarse_terms(image, modes_ref, mask, own_row),
        (
            2.0 * row_sum(projected * image),
            2.0 * row_sum(projected * product) + 2.0 * row_sum(direction * image),
            row_sum(projected * projected),
        ),
    )
    reduce_start(pay_b, first_b, send_b1, receive_b1, own, plane)
    reduce_middle(*round_b)
    direction_rows = permuted(direction, onehot_ref[...], nt)
    projected_rows = permuted(projected, onehot_ref[...], nt)
    order = (
        iota((NC, NC), 1)
        == MODES * jnp.bitwise_and(iota((NC, NC), 0), AGGS - 1) + lax.shift_right_logical(iota((NC, NC), 0), 6)
    ).astype(F32).astype(BF16)
    exchange_sent(message, landed, send_x, receive_x, own, plane)
    reduce_sent(*round_a)
    reduce_finish(*round_b)

    image_coarse, sums = read_result(result_b)
    renewed = sums[:, 2:3]
    ratio = renewed / inner
    bend = sums[:, 0:1] + ratio * sums[:, 1:2] + ratio * ratio * curvature
    step_next = renewed / bend
    coarse_last = coarse_next - step_next * (image_coarse + ratio * coarse_jump)
    final = solved(coarse_last, parts_ref)
    amplitudes_ref[...] = permuted(final, order, nn)
    multipliers_ref[...] = (
        step * direction_rows + step_next * (projected_rows + ratio * direction_rows)
    )
    reduce_sent(*round_b)


VMEM = pl.BlockSpec(memory_space=pltpu.VMEM)
DMA = pltpu.SemaphoreType.DMA


def shape(dims, kind=F32):
    return jax.ShapeDtypeStruct(dims, kind)


def whole_kernel(*refs):
    inputs, outputs = refs[:5], refs[5:7]
    between, setup_work, solve_work = refs[7:16], refs[16:44], refs[44:]
    setup_kernel(*inputs, *between, *setup_work)
    solve_kernel(*between, *outputs, *solve_work)


def body(dual_ops, mode_traces, route, mode_block, local_gap):
    tile = pltpu.VMEM((8, 128), F32)
    many = pltpu.VMEM((SUB, 8, 128), F32)
    few = pltpu.VMEM((TILES, 8, 128), F32)
    between = [
        pltpu.VMEM((CASES, ROWS), F32), pltpu.VMEM((2, 8, ROWS), F32),
        pltpu.VMEM((128, ROWS), BF16), pltpu.VMEM((8, 128), F32),
        pltpu.VMEM((ROWS, ROWS), BF16), pltpu.VMEM((ROWS, ROWS), BF16),
        pltpu.VMEM((NC, NC), F32), pltpu.VMEM((CASES, NC), F32), pltpu.VMEM((CASES, 128), F32),
    ]
    setup_work = [
        many, many,
        pltpu.VMEM((ROWS, ROWS), BF16), pltpu.VMEM((ROWS, ROWS), BF16),
        pltpu.VMEM((AGGS, 1, 128), F32), pltpu.VMEM((SUB, 1, 128), F32),
        pltpu.VMEM((SLICE, 128), F32), pltpu.VMEM((REP, SLICE, 128), F32),
        pltpu.VMEM((SLICE, 128), F32), pltpu.VMEM((AGGS, SLICE, 128), F32),
        DMA((SUB,)), DMA((SUB,)), DMA((SUB,)), DMA((SUB,)),
        DMA((REP,)), DMA((REP,)), DMA((8,)), DMA((8,)),
        DMA((4,)), DMA((4,)), DMA((4,)), DMA((4,)),
        pltpu.VMEM((1, ROWS, ROWS), BF16), pltpu.VMEM((MODES, 1, ROWS), F32),
        pltpu.VMEM((1, ROWS), jnp.int32), pltpu.VMEM((1, SUB * REP), jnp.int32),
        pltpu.VMEM((CASES, ROWS), F32), DMA((5,)),
    ]
    solve_work = (
        [pltpu.VMEM((3, NC, NC), BF16), pltpu.VMEM((NC, NC), F32), many, many]
        + [few, many, tile, few, tile, few] * 2
        + [DMA((SUB,)), DMA((SUB,))]
        + [DMA((TILES,)), DMA((SUB,)), DMA((REP,)), DMA((REP,)), DMA((SUB,)), DMA((TILES,))] * 2
    )
    assert len(setup_work) == 28
    return pl.pallas_call(
        whole_kernel,
        out_shape=(shape((CASES, ROWS)), shape((CASES, NC))),
        in_specs=[pl.BlockSpec(memory_space=pltpu.HBM)] * 5,
        out_specs=(VMEM,) * 2,
        scratch_shapes=between + setup_work + solve_work,
        compiler_params=pltpu.CompilerParams(
            collective_id=0, has_side_effects=True, vmem_limit_bytes=LIMIT
        ),
        name="whole",
    )(
        dual_ops,
        jnp.transpose(mode_traces, (1, 0, 2)),
        route,
        mode_block.reshape(1, SUB * REP),
        local_gap,
    )


def solution(mesh):
    placed = (
        P(("sub", "rep"), None, None),
        P(("sub", "rep"), None, None),
        P(("sub", "rep"), None),
        P(),
        P(None, ("sub", "rep")),
    )
    return jax.shard_map(
        body, mesh=mesh, in_specs=placed, out_specs=(P(None, ("sub", "rep")), P()), check_vma=False
    )
```
